256 devices in a mesh: rows: 16 (over z, core), cols: 16 (over y, x).
Axes of the slice: x: 4, y: 4, z: 8, core: 2. Of those that a mesh axis runs over, the one named last changes fastest.
Arguments:
- window_slab: float32 [24576, 4096], P('rows', 'cols'), may hold values from -6 to 6
- first_inverse: float32 [2, 512, 512], replicated, may hold values from -2 to 2, as said below
- first_factor: float32 [2, 512, 24576], P(None, 'cols', 'rows'), may hold values from -0.25 to 0.25
- second_inverse: float32 [2, 512, 512], replicated, may hold values from -2 to 2, as said below
- second_factor: float32 [2, 512, 4096], P(None, 'cols', 'rows'), may hold values from -0.25 to 0.25
Outputs:
- reduced: float32 [24576, 4096], P('cols', 'rows')
The draws below stay inside these ranges and needn't reach their ends.
Inputs may be any that keep to these rules, and one draw needn't show every extreme that they name: first_inverse[k] is lower triangular with diagonal entries from 0.5 to 2. second_inverse[k] is lower triangular with diagonal entries from 0.5 to 2.
All inputs are finite; a program needn't handle non-finite values.
Results may differ from the reference program's by a relative error of at most 0.0001.
Values sent between devices are 32-bit elements; how exact they have to be, the bound alone decides.
A program may use at most 64 MiB of HBM per device.

```python
import math
import jax
import jax.numpy as jnp
from jax import lax

ORDER = 24576
WIDTH = 4096
PANEL = 512
BLOCK = 128
PANELS = 2
ROW_SHARE = 1536
PIECE = 96
N_ROWS = 16
N_COLS = 16


def triangle(key, salt):
    folded = jax.random.fold_in(key, salt)
    diag_key, off_key = jax.random.split(folded)
    shape = (PANELS, PANEL, PANEL)
    diagonal = jnp.exp(jax.random.uniform(diag_key, shape, jnp.float32, math.log(0.5), math.log(2.0)))
    offdiag = jnp.clip(jax.random.normal(off_key, shape, jnp.float32), -4.0, 4.0) * 0.7 / math.sqrt(PANEL)
    row_ids = lax.broadcasted_iota(jnp.int32, shape, 1)
    col_ids = lax.broadcasted_iota(jnp.int32, shape, 2)
    return jnp.where(row_ids == col_ids, diagonal, jnp.where(row_ids > col_ids, offdiag, 0.0)).astype(jnp.float32)


def draw_first_inverse(key, part):
    return triangle(key, 11)


def draw_second_inverse(key, part):
    return triangle(key, 23)


def shard_levels(rng, shape, pieces, low, top_value):
    level = 1.0
    for position, blocks in pieces:
        heights = jax.random.uniform(jax.random.fold_in(jax.random.fold_in(rng, 6), position), (blocks,), jnp.float32, low / len(pieces), top_value / len(pieces))
        level = level * jnp.repeat(jnp.exp(heights), shape[position] // blocks).reshape((-1,) + (1,) * (len(shape) - 1 - position))
    return level


def centred(own_key, extent, spread, most, cuts=(), held_as=jnp.bfloat16):
    drawn = jax.random.normal(own_key, extent, jnp.float32) * spread
    if len(cuts) > 0:
        drawn = shard_levels(own_key, extent, cuts, -0.22, 0.18) * drawn
    return jnp.clip(drawn, min=-most, max=most).astype(held_as)


def setup_inputs(seed: int = 0) -> dict:
    key_of = jax.random.split(jax.random.key(seed), 6)
    window_slab = centred(key_of[0], (ORDER, WIDTH), 1.0, 6.0, ((0, 16), (1, 16)), jnp.float32)
    first_inverse = draw_first_inverse(jax.random.fold_in(key_of[5], 71), 0)
    first_factor = centred(key_of[2], (PANELS, PANEL, ORDER), PANEL ** -0.5, 0.25, ((1, 16), (2, 16)), jnp.float32)
    second_inverse = draw_second_inverse(jax.random.fold_in(key_of[5], 71), 0)
    second_factor = centred(key_of[4], (PANELS, PANEL, WIDTH), PANEL ** -0.5, 0.25, ((1, 16), (2, 16)), jnp.float32)
    return {"window_slab": window_slab, "first_inverse": first_inverse, "first_factor": first_factor, "second_inverse": second_inverse, "second_factor": second_factor}


HIGHEST = lax.Precision.HIGHEST


def to_logical(stored):
    trailing = stored.shape[1]
    return stored.reshape(N_ROWS, ROW_SHARE // BLOCK, BLOCK, trailing).transpose(1, 0, 2, 3).reshape(ORDER, trailing)


def to_stored(logical):
    trailing = logical.shape[1]
    return logical.reshape(ROW_SHARE // BLOCK, N_ROWS, BLOCK, trailing).transpose(1, 0, 2, 3).reshape(ORDER, trailing)


def reference(window_slab, first_inverse, first_factor, second_inverse, second_factor):
    current = to_logical(window_slab)
    factors = to_logical(first_factor.transpose(2, 0, 1).reshape(ORDER, PANELS * PANEL))
    for panel_index in range(PANELS):
        panel_start = panel_index * PANEL
        panel_end = panel_start + PANEL
        solved = jnp.dot(first_inverse[panel_index], current[panel_start:panel_end], precision=HIGHEST, preferred_element_type=jnp.float32)
        update = jnp.dot(factors[panel_end:, panel_start:panel_end], solved, precision=HIGHEST, preferred_element_type=jnp.float32)
        current = jnp.concatenate([current[:panel_start], solved, current[panel_end:] - update], axis=0)
    turned = to_stored(current).reshape(N_ROWS, N_COLS, PIECE, WIDTH).transpose(1, 0, 2, 3).reshape(ORDER, WIDTH)
    for panel_index in range(PANELS):
        panel_start = panel_index * PANEL
        panel_end = panel_start + PANEL
        solved = jnp.dot(turned[:, panel_start:panel_end], second_inverse[panel_index].T, precision=HIGHEST, preferred_element_type=jnp.float32)
        update = jnp.dot(solved, second_factor[panel_index][:, panel_end:], precision=HIGHEST, preferred_element_type=jnp.float32)
        turned = jnp.concatenate([turned[:, :panel_start], solved, turned[:, panel_end:] - update], axis=1)
    return turned
```

```python
import jax
import jax.numpy as jnp
from jax import lax
from jax.experimental import pallas as pl
from jax.experimental.pallas import tpu as pltpu
from jax.sharding import PartitionSpec as P

MESH = pl.DeviceIdType.MESH
F32 = jnp.float32
BF16 = jnp.bfloat16
NN = (((1,), (0,)), ((), ()))
NT = (((1,), (1,)), ((), ()))


def split(value):
    high = value.astype(BF16)
    return high, (value - high.astype(F32)).astype(BF16)


def product(a, b, dims=NN):
    def dot(u, v):
        return lax.dot_general(u, v, dims, preferred_element_type=F32)

    return dot(a[0], b[0]) + (dot(a[0], b[1]) + dot(a[1], b[0]))


def remote(src, dst, send_sem, recv_sem, device):
    return pltpu.make_async_remote_copy(
        src_ref=src,
        dst_ref=dst,
        send_sem=send_sem,
        recv_sem=recv_sem,
        device_id=device,
        device_id_type=MESH,
    )


class Gather4:
    def __init__(self, index, device, slot, half, send, recv):
        self.up, self.down, self.far = (index + 1) % 4, (index + 3) % 4, (index + 2) % 4
        self.slot = slot
        to_up, to_down = device(self.up), device(self.down)
        own = slot(index)
        self.first = [
            remote(own, own, send.at[0], recv.at[0], to_up),
            remote(own, own, send.at[1], recv.at[1], to_down),
        ]
        self.second = [
            remote(half(0, self.down), half(0, self.down), send.at[2], recv.at[2], to_up),
            remote(half(1, self.up), half(1, self.up), send.at[3], recv.at[3], to_down),
        ]
        self.landing = [
            remote(own, slot(self.down), send.at[0], recv.at[0], to_up),
            remote(own, slot(self.up), send.at[1], recv.at[1], to_down),
            remote(half(0, self.far), half(0, self.far), send.at[2], recv.at[2], to_up),
            remote(half(1, self.far), half(1, self.far), send.at[3], recv.at[3], to_down),
        ]

    def start(self):
        for copy in self.first:
            copy.start()

    def forward(self, then=None):
        for way in (0, 1):
            self.landing[way].wait_recv()
            self.second[way].start()
            if then is not None:
                then(way, (self.down, self.up)[way])

    def finish(self, then=None):
        self.landing[2].wait_recv()
        self.landing[3].wait_recv()
        if then is not None:
            then(2, self.far)

    def drain(self):
        for copy in self.first + self.second:
            copy.wait_send()


class Ring8:
    def __init__(self, z, step, device, is_source, block, send, recv, then=None):
        self.z, self.step_by, self.is_source = z, step, is_source
        self.block, self.send, self.recv, self.then = block, send, recv, then
        self.following = device((z + 8 + step) % 8)

    def copy(self, source, src=None):
        block = self.block(source)
        return remote(
            block if src is None else src,
            block,
            self.send.at[source],
            self.recv.at[source],
            self.following,
        )

    def begin(self, src=None):
        @pl.when(self.is_source(self.z))
        def _():
            self.copy(self.z, src).start()

    def hop(self, count):
        source = (self.z + 16 - self.step_by * count) % 8

        @pl.when(self.is_source(source))
        def _():
            self.copy(source).wait_recv()
            if count < 7:
                self.copy(source).start()
            if self.then is not None:
                self.then(source)

    def drain(self):
        for count in range(7):
            source = (self.z + 16 - self.step_by * count) % 8

            @pl.when(self.is_source(source))
            def _():
                self.copy(source).wait_send()


def kernel(
    slab,
    inverse1,
    factor1,
    inverse2,
    factor2,
    out,
    i1,
    i2,
    xt,
    xp,
    fx,
    gx,
    ft,
    wh,
    wl,
    sb,
    sh,
    sl,
    gt,
    pb,
    zf,
    zh,
    zl,
    db,
    local,
    xp_send,
    xp_recv,
    xs_send,
    xs_recv,
    fz_send,
    fz_recv,
    gz_send,
    gz_recv,
    fxx_send,
    fxx_recv,
    fxy_send,
    fxy_recv,
    gxx_send,
    gxx_recv,
    gxy_send,
    gxy_recv,
    sib_send,
    sib_recv,
    fa_send,
    fa_recv,
    ft_send,
    ft_recv,
    xa_send,
    xa_recv,
    ga_send,
    ga_recv,
    gr_send,
    gr_recv,
    gy_send,
    gy_recv,
    gs_send,
    gs_recv,
    s_send,
    s_recv,
    ss_send,
    ss_recv,
    p_send,
    p_recv,
    o_send,
    o_recv,
):
    r = lax.axis_index("rows")
    c = lax.axis_index("cols")
    z, k = r // 2, r % 2
    y, x = c // 4, c % 4
    way = 1 - 2 * k
    sibling = (2 * z + 1 - k, c)

    def along_y(index):
        return (r, 4 * index + x)

    def along_x(index):
        return (r, 4 * y + index)

    def along_z(index):
        return (2 * index + k, c)

    panel_rows = slab.at[pl.ds(0, 128), :]

    def xp_block(source):
        return xp.at[2 * source + k]

    def xp_to_sibling(source, src=None):
        block = xp_block(source)
        return remote(
            block if src is None else src, block, xs_send.at[source], xs_recv.at[source], sibling
        )

    def in_panels(source):
        return source < 4

    panels = Ring8(
        z,
        way,
        along_z,
        in_panels,
        xp_block,
        xp_send,
        xp_recv,
        then=lambda source: xp_to_sibling(source).start(),
    )
    panels.begin(panel_rows)

    def own_panel():
        return pltpu.make_async_copy(panel_rows, xp_block(z), local.at[0])

    @pl.when(in_panels(z))
    def _():
        xp_to_sibling(z, panel_rows).start()
        own_panel().start()

    fz_src = factor1.at[0, :, pl.ds(0, 128)]
    gz_src = factor2.at[0]

    def fz_dst(which):
        return fx.at[k, which, y, x]

    gz_dst = gx.at[k, y, x]
    fz_own = pltpu.make_async_copy(fz_src, fz_dst((z + 6) % 2), local.at[1])
    gz_own = pltpu.make_async_copy(gz_src, gz_dst, local.at[2])
    f_source = jnp.logical_or(z == 2, z == 3)

    def fz_copy(distance):
        return remote(
            fz_src,
            fz_dst(z % 2),
            fz_send.at[distance - 1],
            fz_recv.at[z % 2],
            along_z((z + distance) % 8),
        )

    def gz_copy(distance):
        return remote(
            gz_src, gz_dst, gz_send.at[distance - 1], gz_recv.at[0], along_z((z + distance) % 8)
        )

    @pl.when(f_source)
    def _():
        fz_own.start()
        for distance in range(1, 8):
            fz_copy(distance).start()

    @pl.when(z == 1)
    def _():
        gz_own.start()
        for distance in range(1, 8):
            gz_copy(distance).start()

    def fa_copy(distance):
        to = (y + distance) % 4
        columns = pl.ds(pl.multiple_of(to * 384, 128), 384)
        return remote(
            factor1.at[:, :, columns],
            ft.at[:, y, x],
            fa_send.at[distance - 1],
            fa_recv.at[distance - 1],
            along_y(to),
        )

    fa_own = pltpu.make_async_copy(
        factor1.at[:, :, pl.ds(pl.multiple_of(y * 384, 128), 384)], ft.at[:, y, x], local.at[3]
    )
    fa_own.start()
    for distance in (1, 3, 2):
        fa_copy(distance).start()

    def xa_copy(distance):
        to = (y + distance) % 4
        return remote(
            slab.at[pl.ds(pl.multiple_of(to * 384, 128), 384), :],
            xt.at[y],
            xa_send.at[distance - 1],
            xa_recv.at[distance - 1],
            along_y(to),
        )

    xa_own = pltpu.make_async_copy(
        slab.at[pl.ds(pl.multiple_of(y * 384, 128), 384), :], xt.at[y], local.at[4]
    )
    xa_own.start()
    for distance in (1, 3, 2):
        xa_copy(distance).start()

    load1 = pltpu.make_async_copy(inverse1, i1, local.at[5])
    load2 = pltpu.make_async_copy(inverse2, i2, local.at[6])
    load1.start()
    load2.start()

    g_plane = r % 4
    g_block = r // 4

    def ga_copy(panel):
        return remote(
            factor2.at[panel],
            gt.at[g_block - 1, panel, y, x],
            ga_send.at[panel],
            ga_recv.at[x, k],
            (2 * z + panel, 4 * y + g_plane),
        )

    def ga_own(panel):
        return pltpu.make_async_copy(
            factor2.at[panel], gt.at[g_block - 1, panel, y, x], local.at[7]
        )

    def ga_stays(panel):
        return jnp.logical_and(g_plane == x, k == panel)

    for panel in (0, 1):

        @pl.when(jnp.logical_and(z >= 2, ga_stays(panel)))
        def _():
            ga_own(panel).start()

        @pl.when(jnp.logical_and(z >= 2, jnp.logical_not(ga_stays(panel))))
        def _():
            ga_copy(panel).start()

    def g_source(source):
        return jnp.logical_and(source >= 2, source % 2 == x // 2)

    g_ring = Ring8(
        z,
        way,
        along_z,
        g_source,
        lambda source: gt.at[source // 2 - 1, k, y],
        gr_send,
        gr_recv,
    )

    def g_slot(index):
        return gt.at[:, k, index]

    def g_to_sibling(number, index):
        return remote(g_slot(index), g_slot(index), gs_send.at[number], gs_recv.at[number], sibling)

    def g_from_sibling(number, index):
        theirs = gt.at[:, 1 - k, index]
        return remote(theirs, theirs, gs_send.at[number], gs_recv.at[number], sibling)

    g_gather = Gather4(
        y,
        along_y,
        g_slot,
        lambda part, index: gt.at[:, k, index, pl.ds(2 * part, 2)],
        gy_send,
        gy_recv,
    )

    fxx = Gather4(
        x,
        along_x,
        lambda index: fx.at[k, :, y, index],
        lambda part, index: fx.at[k, part, y, index],
        fxx_send,
        fxx_recv,
    )
    fxy = Gather4(
        y,
        along_y,
        lambda index: fx.at[k, :, index],
        lambda part, index: fx.at[k, part, index],
        fxy_send,
        fxy_recv,
    )
    gxx = Gather4(
        x,
        along_x,
        lambda index: gx.at[k, y, index],
        lambda part, index: gx.at[k, y, index, pl.ds(16 * part, 16)],
        gxx_send,
        gxx_recv,
    )
    gxy = Gather4(
        y,
        along_y,
        lambda index: gx.at[k, index],
        lambda part, index: gx.at[k, index, pl.ds(2 * part, 2)],
        gxy_send,
        gxy_recv,
    )
    fx_to_sibling = remote(fx.at[k], fx.at[k], sib_send.at[0], sib_recv.at[0], sibling)
    gx_to_sibling = remote(gx.at[k], gx.at[k], sib_send.at[1], sib_recv.at[1], sibling)
    fx_from_sibling = remote(fx.at[1 - k], fx.at[1 - k], sib_send.at[0], sib_recv.at[0], sibling)
    gx_from_sibling = remote(gx.at[1 - k], gx.at[1 - k], sib_send.at[1], sib_recv.at[1], sibling)

    for which in (0, 1):

        @pl.when(z == 2 + which)
        def _():
            fz_own.wait()

        @pl.when(z != 2 + which)
        def _():
            remote(
                fz_src, fz_dst(which), fz_send.at[0], fz_recv.at[which], sibling
            ).wait_recv()

    @pl.when(z == 1)
    def _():
        gz_own.wait()

    @pl.when(z != 1)
    def _():
        remote(gz_src, gz_dst, gz_send.at[0], gz_recv.at[0], sibling).wait_recv()

    fxx.start()
    gxx.start()
    panels.hop(1)
    fxx.forward()
    gxx.forward()
    panels.hop(2)
    fxx.finish()
    fxy.start()
    gxx.finish()
    gxy.start()
    panels.hop(3)
    fxy.forward()
    gxy.forward()
    panels.hop(4)
    fxy.finish()
    fx_to_sibling.start()
    gxy.finish()
    gx_to_sibling.start()
    panels.hop(5)

    f_gather = Gather4(
        x,
        along_x,
        lambda index: ft.at[:, :, index],
        lambda part, index: ft.at[part, :, index],
        ft_send,
        ft_recv,
    )
    fa_own.wait()
    for distance in (1, 3, 2):
        remote(
            ft.at[:, y, x],
            ft.at[:, (y + 4 - distance) % 4, x],
            fa_send.at[distance - 1],
            fa_recv.at[distance - 1],
            sibling,
        ).wait_recv()
    f_gather.start()
    panels.hop(6)

    @pl.when(g_source(z))
    def _():
        for source_x in range(4):
            stays = jnp.logical_and(source_x == x, k == x % 2)
            block = gt.at[z // 2 - 1, k, y, source_x]

            @pl.when(stays)
            def _():
                pltpu.make_async_copy(factor2.at[k], block, local.at[7]).wait()

            @pl.when(jnp.logical_not(stays))
            def _():
                remote(
                    block, block, ga_send.at[0], ga_recv.at[source_x, x % 2], sibling
                ).wait_recv()

    g_ring.begin()
    panels.hop(7)
    f_gather.forward()

    @pl.when(in_panels(z))
    def _():
        own_panel().wait()

    for source in range(4):
        block = xp.at[2 * source + 1 - k]
        remote(block, block, xs_send.at[source], xs_recv.at[source], sibling).wait_recv()
    load1.wait()

    s_gather = Gather4(
        y,
        along_y,
        lambda index: sb.at[index, k],
        lambda part, index: sb.at[index, k, pl.ds(256 * part, 256)],
        s_send,
        s_recv,
    )

    def s_to_sibling(number, index):
        block = sb.at[index, k]
        return remote(block, block, ss_send.at[number], ss_recv.at[number], sibling)

    def s_from_sibling(number, index):
        block = sb.at[index, 1 - k]
        return remote(block, block, ss_send.at[number], ss_recv.at[number], sibling)

    raw0 = split(xp[pl.ds(0, 4)].reshape(512, 256))
    solved0 = product(split(i1[0]), raw0)
    sb[y, 0] = solved0
    sh[...], sl[...] = split(solved0)

    @pl.when(k == 0)
    def _():
        s_gather.start()

    g_ring.hop(1)
    fx_from_sibling.wait_recv()
    remaining = []
    for number in range(4):
        coupling = split(fx[number % 2, number // 2].reshape(512, 128).T)
        remaining.append(xp[4 + number] - product(coupling, (sh[...], sl[...])))
    solved1 = product(split(i1[1]), split(jnp.concatenate(remaining, axis=0)))
    sb[y, 1] = solved1

    @pl.when(k == 1)
    def _():
        s_gather.start()

    f_gather.finish()
    for panel in (0, 1):
        for part in range(4):
            high, rest = split(ft[panel, part].reshape(128, 384).T)
            at = (4 * panel + part) * 128
            wh[:, at : at + 128] = high
            wl[:, at : at + 128] = rest
    g_ring.hop(2)
    s_gather.forward(then=lambda number, index: s_to_sibling(number, index).start())
    g_ring.hop(3)
    g_ring.hop(4)
    s_gather.finish(then=lambda number, index: s_to_sibling(number, index).start())
    g_ring.hop(5)
    xa_own.wait()
    for distance in (1, 3, 2):
        remote(
            xt.at[y],
            xt.at[(y + 4 - distance) % 4],
            xa_send.at[distance - 1],
            xa_recv.at[distance - 1],
            sibling,
        ).wait_recv()
    for number, index in ((0, s_gather.down), (1, s_gather.up), (2, s_gather.far)):
        s_from_sibling(number, index).wait_recv()

    has_panel_rows = jnp.logical_and(y == 0, r < 8)
    own_rows = pl.ds(pl.multiple_of((r % 4) * 128, 128), 128)
    own_panel_index = (r // 4) % 2

    def left(block):
        solved = split(sb[block].reshape(1024, 256))
        return xt[block] - product((wh[...], wl[...]), solved)

    pb[x] = left(0)

    @pl.when(has_panel_rows)
    def _():
        pb[x, pl.ds(0, 128)] = sb[0, own_panel_index, own_rows]

    p_gather = Gather4(
        x,
        along_x,
        lambda index: pb.at[index],
        lambda part, index: pb.at[index, pl.ds(192 * part, 192)],
        p_send,
        p_recv,
    )
    p_gather.start()
    g_ring.hop(6)
    g_ring.hop(7)
    g_gather.start()
    g_to_sibling(3, y).start()

    @pl.loop(1, 4)
    def _(block):
        db[block - 1] = left(block)

        @pl.when(has_panel_rows)
        def _():
            db[block - 1, pl.ds(0, 128)] = sb[block, own_panel_index, own_rows]

    p_gather.forward()
    g_gather.forward(then=lambda number, index: g_to_sibling(number, index).start())
    p_gather.finish()

    load2.wait()
    gx_from_sibling.wait_recv()

    def solve_columns(panel, first):
        total = None
        for part in (0, 1):
            term = product(
                first(part), split(i2[panel, :, 256 * part : 256 * part + 256]), NT
            )
            total = term if total is None else total + term
        for part in (0, 1):
            value = total[:, 256 * part : 256 * part + 256]
            zf[2 * panel + part] = value
            at = 512 * panel + 256 * part
            zh[:, at : at + 256], zl[:, at : at + 256] = split(value)

    def out_copy(block, piece, src):
        return remote(
            src,
            out.at[pl.ds(pl.multiple_of(r * 96, 96), 96), :],
            o_send.at[block, piece],
            o_recv.at[r],
            (4 * block + x, 4 * y + piece),
        )

    def out_own(src):
        return pltpu.make_async_copy(
            src, out.at[pl.ds(pl.multiple_of(r * 96, 96), 96), :], local.at[8]
        )

    def for_pieces(block, values, remote_do, local_do):
        for piece in range(4):
            src = values.at[pl.ds(96 * piece, 96)]
            stays = jnp.logical_and(4 * block + x == r, x == piece)

            @pl.when(stays)
            def _():
                local_do(out_own(src))

            @pl.when(jnp.logical_not(stays))
            def _():
                remote_do(out_copy(block, piece, src))

    def start(copy):
        copy.start()

    solve_columns(0, lambda part: split(pb[part]))
    g_gather.finish(then=lambda number, index: g_to_sibling(number, index).start())
    solved_cols = (zh[:, :512], zl[:, :512])
    remaining = []
    for part in (0, 1):
        coupling = split(gx[part].reshape(512, 256))
        remaining.append(split(pb[2 + part] - product(solved_cols, coupling)))
    solve_columns(1, lambda part: remaining[part])
    for_pieces(0, zf.at[x], start, start)

    for number, index in ((0, g_gather.down), (1, g_gather.up), (2, g_gather.far)):
        g_from_sibling(number, index).wait_recv()
    g_from_sibling(3, y).wait_recv()
    for block in range(1, 4):
        factor = split(gt[block - 1].reshape(1024, 256))
        db[block - 1] = db[block - 1] - product((zh[...], zl[...]), factor)
        for_pieces(block, db.at[block - 1], start, start)

    for source in range(16):
        stays = jnp.logical_and(source == r, x == r % 4)
        rows = out.at[pl.ds(96 * source, 96), :]

        @pl.when(jnp.logical_not(stays))
        def _():
            remote(rows, rows, o_send.at[0, 0], o_recv.at[source], sibling).wait_recv()

    for block in range(4):
        for_pieces(
            block,
            zf.at[x] if block == 0 else db.at[block - 1],
            lambda copy: copy.wait_send(),
            lambda copy: copy.wait(),
        )
    panels.drain()
    g_ring.drain()

    @pl.when(in_panels(z))
    def _():
        xp_to_sibling(z).wait_send()

    for count in range(1, 8):
        source = (z + 16 - way * count) % 8

        @pl.when(in_panels(source))
        def _():
            xp_to_sibling(source).wait_send()

    @pl.when(f_source)
    def _():
        for distance in range(1, 8):
            fz_copy(distance).wait_send()

    @pl.when(z == 1)
    def _():
        for distance in range(1, 8):
            gz_copy(distance).wait_send()

    for distance in (1, 2, 3):
        fa_copy(distance).wait_send()
        xa_copy(distance).wait_send()
    for panel in (0, 1):

        @pl.when(jnp.logical_and(z >= 2, jnp.logical_not(ga_stays(panel))))
        def _():
            ga_copy(panel).wait_send()

    for gather in (fxx, fxy, gxx, gxy, f_gather, s_gather, p_gather, g_gather):
        gather.drain()
    fx_to_sibling.wait_send()
    gx_to_sibling.wait_send()
    for number, index in ((0, s_gather.down), (1, s_gather.up), (2, s_gather.far)):
        s_to_sibling(number, index).wait_send()
        g_to_sibling(number, index).wait_send()
    g_to_sibling(3, y).wait_send()


def on_device(*arrays):
    dma = pltpu.SemaphoreType.DMA
    any_space = pl.BlockSpec(memory_space=pl.ANY)
    scratch = [
        pltpu.VMEM((2, 512, 512), F32),
        pltpu.VMEM((2, 512, 512), F32),
        pltpu.VMEM((4, 384, 256), F32),
        pltpu.VMEM((8, 128, 256), F32),
        pltpu.VMEM((2, 2, 4, 4, 32, 128), F32),
        pltpu.VMEM((2, 4, 4, 32, 256), F32),
        pltpu.VMEM((2, 4, 4, 32, 384), F32),
        pltpu.VMEM((384, 1024), BF16),
        pltpu.VMEM((384, 1024), BF16),
        pltpu.VMEM((4, 2, 512, 256), F32),
        pltpu.VMEM((512, 256), BF16),
        pltpu.VMEM((512, 256), BF16),
        pltpu.VMEM((3, 2, 4, 4, 32, 256), F32),
        pltpu.VMEM((4, 384, 256), F32),
        pltpu.VMEM((4, 384, 256), F32),
        pltpu.VMEM((384, 1024), BF16),
        pltpu.VMEM((384, 1024), BF16),
        pltpu.VMEM((3, 384, 256), F32),
        dma((9,)),
        dma((8,)),
        dma((8,)),
        dma((4,)),
        dma((4,)),
        dma((7,)),
        dma((2,)),
        dma((7,)),
        dma((1,)),
        dma((4,)),
        dma((4,)),
        dma((4,)),
        dma((4,)),
        dma((4,)),
        dma((4,)),
        dma((4,)),
        dma((4,)),
        dma((2,)),
        dma((2,)),
        dma((3,)),
        dma((3,)),
        dma((4,)),
        dma((4,)),
        dma((3,)),
        dma((3,)),
        dma((2,)),
        dma((4, 2)),
        dma((8,)),
        dma((8,)),
        dma((4,)),
        dma((4,)),
        dma((4,)),
        dma((4,)),
        dma((4,)),
        dma((4,)),
        dma((3,)),
        dma((3,)),
        dma((4,)),
        dma((4,)),
        dma((4, 4)),
        dma((16,)),
    ]
    return pl.pallas_call(
        kernel,
        out_shape=jax.ShapeDtypeStruct((1536, 256), F32),
        in_specs=[any_space] * 5,
        out_specs=any_space,
        scratch_shapes=scratch,
        compiler_params=pltpu.CompilerParams(
            has_side_effects=True, vmem_limit_bytes=56 * 1024 * 1024
        ),
        name="two_sided_panels",
    )(*arrays)


def solution(mesh):
    return jax.shard_map(
        on_device,
        mesh=mesh,
        in_specs=(P("rows", "cols"), P(), P(None, "cols", "rows"), P(), P(None, "cols", "rows")),
        out_specs=P("cols", "rows"),
        check_vma=False,
    )
```

```python
import jax
import jax.numpy as jnp
from jax import lax
from jax.experimental import pallas as pl
from jax.experimental.pallas import tpu as pltpu
from jax.sharding import PartitionSpec as P

MESH = pl.DeviceIdType.MESH
F32 = jnp.float32
BF16 = jnp.bfloat16
NN = (((1,), (0,)), ((), ()))
NT = (((1,), (1,)), ((), ()))


def split(value):
    high = value.astype(BF16)
    return high, (value - high.astype(F32)).astype(BF16)


def product(a, b, dims=NN):
    def dot(u, v):
        return lax.dot_general(u, v, dims, preferred_element_type=F32)

    return dot(a[0], b[0]) + (dot(a[0], b[1]) + dot(a[1], b[0]))


def remote(src, dst, send_sem, recv_sem, device):
    return pltpu.make_async_remote_copy(
        src_ref=src,
        dst_ref=dst,
        send_sem=send_sem,
        recv_sem=recv_sem,
        device_id=device,
        device_id_type=MESH,
    )


class Gather4:
    def __init__(self, index, device, slot, half, send, recv, src=None):
        self.up, self.down, self.far = (index + 1) % 4, (index + 3) % 4, (index + 2) % 4
        self.slot = slot
        to_up, to_down = device(self.up), device(self.down)
        own = slot(index)
        self.first = [
            remote(own if src is None else src, own, send.at[0], recv.at[0], to_up),
            remote(own if src is None else src, own, send.at[1], recv.at[1], to_down),
        ]
        self.second = [
            remote(half(0, self.down), half(0, self.down), send.at[2], recv.at[2], to_up),
            remote(half(1, self.up), half(1, self.up), send.at[3], recv.at[3], to_down),
        ]
        self.landing = [
            remote(own, slot(self.down), send.at[0], recv.at[0], to_up),
            remote(own, slot(self.up), send.at[1], recv.at[1], to_down),
            remote(half(0, self.far), half(0, self.far), send.at[2], recv.at[2], to_up),
            remote(half(1, self.far), half(1, self.far), send.at[3], recv.at[3], to_down),
        ]

    def start(self):
        for copy in self.first:
            copy.start()

    def forward(self, then=None):
        for way in (0, 1):
            self.landing[way].wait_recv()
            self.second[way].start()
            if then is not None:
                then(way, (self.down, self.up)[way])

    def finish(self, then=None):
        self.landing[2].wait_recv()
        self.landing[3].wait_recv()
        if then is not None:
            then(2, self.far)

    def drain(self):
        for copy in self.first + self.second:
            copy.wait_send()


class Spread8:
    def __init__(self, z, device, is_source, block, up, down):
        self.z, self.is_source, self.block, self.up, self.down = z, is_source, block, up, down
        self.above, self.below = device((z + 1) % 8), device((z + 7) % 8)

    def source(self, event):
        return (self.z + 16 - event) % 8

    def copy(self, way, source, src=None):
        block = self.block(source)
        send, recv = self.up if way > 0 else self.down
        to = self.above if way > 0 else self.below
        return remote(
            block if src is None else src, block, send.at[source], recv.at[source], to
        )

    def landed(self, event, then=None, src=None):
        source = self.source(event)

        @pl.when(self.is_source(source))
        def _():
            if event != 0:
                self.copy(1 if event > 0 else -1, source).wait_recv()
            if 0 <= event < 4:
                self.copy(1, source, src).start()
            if -3 < event <= 0:
                self.copy(-1, source, src).start()
            if then is not None:
                then(source)

    def sent(self, event, then=None):
        source = self.source(event)

        @pl.when(self.is_source(source))
        def _():
            if 0 <= event < 4:
                self.copy(1, source).wait_send()
            if -3 < event <= 0:
                self.copy(-1, source).wait_send()
            if then is not None:
                then(source)


EVENTS = (0, 1, -1, 2, -2, 3, -3, 4)


def kernel(
    slab,
    inverse1,
    factor1,
    inverse2,
    factor2,
    out,
    i1,
    i2h,
    i2l,
    kh,
    kl,
    xt,
    xp,
    fx,
    gx,
    ft,
    wh,
    wl,
    vh,
    vl,
    gt,
    pb,
    zh,
    zl,
    db,
    eb,
    local,
    up_send,
    up_recv,
    down_send,
    down_recv,
    py_send,
    py_recv,
    xs_send,
    xs_recv,
    fz_send,
    fz_recv,
    gz_send,
    gz_recv,
    fxx_send,
    fxx_recv,
    fxy_send,
    fxy_recv,
    gxx_send,
    gxx_recv,
    gxy_send,
    gxy_recv,
    sib_send,
    sib_recv,
    fa_send,
    fa_recv,
    ft_send,
    ft_recv,
    xa_send,
    xa_recv,
    ga_send,
    ga_recv,
    gu_send,
    gu_recv,
    gd_send,
    gd_recv,
    gy_send,
    gy_recv,
    gs_send,
    gs_recv,
    p_send,
    p_recv,
    e_send,
    e_recv,
    o_send,
    o_recv,
):
    r = lax.axis_index("rows")
    c = lax.axis_index("cols")
    z, k = r // 2, r % 2
    y, x = c // 4, c % 4
    sibling = (2 * z + 1 - k, c)
    scope = jax.named_scope

    def along_y(index):
        return (r, 4 * index + x)

    def along_x(index):
        return (r, 4 * y + index)

    def along_z(index):
        return (2 * index + k, c)

    panel_rows = slab.at[pl.ds(0, 128), :]

    def in_panels(source):
        return source < 4

    def block_of(index, source, core=k):
        return xp.at[index, 2 * source + core]

    def xs_copy(number, index, source, src=None):
        block = block_of(index, source)
        return remote(
            block if src is None else src,
            block,
            xs_send.at[number, source],
            xs_recv.at[number, source],
            sibling,
        )

    def xs_landing(number, index, source):
        block = block_of(index, source, 1 - k)
        return remote(
            block, block, xs_send.at[number, source], xs_recv.at[number, source], sibling
        )

    def over_y(source, src=None):
        return Gather4(
            y,
            along_y,
            lambda index: block_of(index, source),
            lambda part, index: xp.at[index, 2 * source + k, pl.ds(64 * part, 64)],
            py_send.at[source],
            py_recv.at[source],
            src,
        )

    panels = Spread8(
        z,
        along_z,
        in_panels,
        lambda source: block_of(y, source),
        (up_send, up_recv),
        (down_send, down_recv),
    )

    def landed(event):
        src = panel_rows if event == 0 else None

        def then(source):
            over_y(source, src).start()
            xs_copy(0, y, source, src).start()

        panels.landed(event, then, src)

    def passed_on(event):
        source = panels.source(event)

        @pl.when(in_panels(source))
        def _():
            over_y(source).forward(
                then=lambda number, index: xs_copy(1 + number, index, source).start()
            )

    def arrived(event):
        source = panels.source(event)

        @pl.when(in_panels(source))
        def _():
            over_y(source).finish(
                then=lambda number, index: xs_copy(1 + number, index, source).start()
            )

    def sent(event):
        def then(source):
            over_y(source).drain()
            for number, index in ((0, y), (1, (y + 3) % 4), (2, (y + 1) % 4), (3, (y + 2) % 4)):
                xs_copy(number, index, source).wait_send()

        panels.sent(event, then)

    def own_panel():
        return pltpu.make_async_copy(panel_rows, block_of(y, z), local.at[0])

    with scope("barrier"):
        barrier = pltpu.get_barrier_semaphore()
        for distance in range(1, 4):
            over_x = (x + distance) % 4
            for device in (
                along_y((y + distance) % 4),
                along_x(over_x),
                (2 * z + 1 - k, 4 * y + over_x),
            ):
                pl.semaphore_signal(barrier, inc=1, device_id=device, device_id_type=MESH)
        for distance in range(1, 16):
            pl.semaphore_signal(
                barrier, inc=1, device_id=((r + distance) % 16, c), device_id_type=MESH
            )
        pl.semaphore_wait(barrier, 24)

    landed(0)

    @pl.when(in_panels(z))
    def _():
        own_panel().start()

    fz_src = factor1.at[0, :, pl.ds(0, 128)]
    gz_src = factor2.at[0]

    def fz_dst(which):
        return fx.at[k, which, y, x]

    gz_dst = gx.at[k, y, x]
    fz_own = pltpu.make_async_copy(fz_src, fz_dst(z % 2), local.at[1])
    gz_own = pltpu.make_async_copy(gz_src, gz_dst, local.at[2])
    f_source = jnp.logical_or(z == 2, z == 3)

    def fz_copy(distance):
        return remote(
            fz_src,
            fz_dst(z % 2),
            fz_send.at[distance - 1],
            fz_recv.at[z % 2],
            along_z((z + distance) % 8),
        )

    def gz_copy(distance):
        return remote(
            gz_src, gz_dst, gz_send.at[distance - 1], gz_recv.at[0], along_z((z + distance) % 8)
        )

    @pl.when(f_source)
    def _():
        fz_own.start()
        for distance in range(1, 8):
            fz_copy(distance).start()

    def fa_copy(distance):
        to = (y + distance) % 4
        columns = pl.ds(pl.multiple_of(to * 384, 128), 384)
        return remote(
            factor1.at[:, :, columns],
            ft.at[:, y, x],
            fa_send.at[distance - 1],
            fa_recv.at[distance - 1],
            along_y(to),
        )

    fa_own = pltpu.make_async_copy(
        factor1.at[:, :, pl.ds(pl.multiple_of(y * 384, 128), 384)], ft.at[:, y, x], local.at[3]
    )
    fa_own.start()
    for distance in (2, 1, 3):
        fa_copy(distance).start()

    load1 = pltpu.make_async_copy(inverse1, i1, local.at[5])
    load1.start()

    @pl.when(z == 1)
    def _():
        gz_own.start()
        for distance in range(1, 8):
            gz_copy(distance).start()

    g_plane = r % 4
    g_block = r // 4

    def ga_copy(panel):
        return remote(
            factor2.at[panel],
            gt.at[g_block - 1, panel, y, x],
            ga_send.at[panel],
            ga_recv.at[x, k],
            (2 * z + panel, 4 * y + g_plane),
        )

    def ga_own(panel):
        return pltpu.make_async_copy(
            factor2.at[panel], gt.at[g_block - 1, panel, y, x], local.at[7]
        )

    def ga_stays(panel):
        return jnp.logical_and(g_plane == x, k == panel)

    for panel in (0, 1):

        @pl.when(jnp.logical_and(z >= 2, ga_stays(panel)))
        def _():
            ga_own(panel).start()

        @pl.when(jnp.logical_and(z >= 2, jnp.logical_not(ga_stays(panel))))
        def _():
            ga_copy(panel).start()

    def g_source(source):
        return jnp.logical_and(source >= 2, source % 2 == x // 2)

    g_spread = Spread8(
        z,
        along_z,
        g_source,
        lambda source: gt.at[source // 2 - 1, k, y],
        (gu_send, gu_recv),
        (gd_send, gd_recv),
    )

    def g_slot(index):
        return gt.at[:, k, index]

    def g_to_sibling(number, index):
        return remote(g_slot(index), g_slot(index), gs_send.at[number], gs_recv.at[number], sibling)

    def g_from_sibling(number, index):
        theirs = gt.at[:, 1 - k, index]
        return remote(theirs, theirs, gs_send.at[number], gs_recv.at[number], sibling)

    g_gather = Gather4(
        y,
        along_y,
        g_slot,
        lambda part, index: gt.at[:, k, index, pl.ds(2 * part, 2)],
        gy_send,
        gy_recv,
    )

    def xa_copy(distance):
        to = (y + distance) % 4
        return remote(
            slab.at[pl.ds(pl.multiple_of(to * 384, 128), 384), :],
            xt.at[y],
            xa_send.at[distance - 1],
            xa_recv.at[distance - 1],
            along_y(to),
        )

    xa_own = pltpu.make_async_copy(
        slab.at[pl.ds(pl.multiple_of(y * 384, 128), 384), :], xt.at[y], local.at[4]
    )

    fxy = Gather4(
        y,
        along_y,
        lambda index: fx.at[k, :, index, x],
        lambda part, index: fx.at[k, part, index, x],
        fxy_send,
        fxy_recv,
    )
    fxx = Gather4(
        x,
        along_x,
        lambda index: fx.at[k, :, :, index],
        lambda part, index: fx.at[k, part, :, index],
        fxx_send,
        fxx_recv,
    )
    gxy = Gather4(
        y,
        along_y,
        lambda index: gx.at[k, index, x],
        lambda part, index: gx.at[k, index, x, pl.ds(16 * part, 16)],
        gxy_send,
        gxy_recv,
    )
    gxx = Gather4(
        x,
        along_x,
        lambda index: gx.at[k, :, index],
        lambda part, index: gx.at[k, pl.ds(2 * part, 2), index],
        gxx_send,
        gxx_recv,
    )
    f_gather = Gather4(
        x,
        along_x,
        lambda index: ft.at[:, :, index],
        lambda part, index: ft.at[part, :, index],
        ft_send,
        ft_recv,
    )
    fx_to_sibling = remote(fx.at[k], fx.at[k], sib_send.at[0], sib_recv.at[0], sibling)
    gx_to_sibling = remote(gx.at[k], gx.at[k], sib_send.at[1], sib_recv.at[1], sibling)
    fx_from_sibling = remote(fx.at[1 - k], fx.at[1 - k], sib_send.at[0], sib_recv.at[0], sibling)
    gx_from_sibling = remote(gx.at[1 - k], gx.at[1 - k], sib_send.at[1], sib_recv.at[1], sibling)

    with scope("wait_panels_1"):
        landed(1)
        landed(-1)
    with scope("pass_panels_0"):
        passed_on(0)
    with scope("wait_coupling_z"):
        for which in (0, 1):

            @pl.when(z == 2 + which)
            def _():
                fz_own.wait()

            @pl.when(z != 2 + which)
            def _():
                remote(
                    fz_src, fz_dst(which), fz_send.at[0], fz_recv.at[which], sibling
                ).wait_recv()

        fxy.start()

        @pl.when(z == 1)
        def _():
            gz_own.wait()

        @pl.when(z != 1)
        def _():
            remote(gz_src, gz_dst, gz_send.at[0], gz_recv.at[0], sibling).wait_recv()

        gxy.start()
    with scope("wait_panels_2"):
        landed(2)
        landed(-2)
    with scope("pass_panels_1"):
        passed_on(1)
        passed_on(-1)
    with scope("wait_first_factor_y"):
        fa_own.wait()
        for distance in (1, 3, 2):
            remote(
                ft.at[:, y, x],
                ft.at[:, (y + 4 - distance) % 4, x],
                fa_send.at[distance - 1],
                fa_recv.at[distance - 1],
                sibling,
            ).wait_recv()
    f_gather.start()
    with scope("pass_coupling_y"):
        fxy.forward()
        gxy.forward()
    with scope("wait_panels_3"):
        landed(3)
        landed(-3)
    with scope("pass_panels_2"):
        passed_on(2)
        passed_on(-2)
    xa_own.start()

    @pl.when(y == 0)
    def _():
        for distance in (2, 1, 3):
            xa_copy(distance).start()

    with scope("finish_coupling_y"):
        fxy.finish()
        fxx.start()
        gxy.finish()
        gxx.start()
    with scope("wait_panels_4"):
        landed(4)
    with scope("pass_panels_3"):
        passed_on(3)
        passed_on(-3)
    with scope("wait_second_factor_x"):

        @pl.when(g_source(z))
        def _():
            for source_x in range(4):
                stays = jnp.logical_and(source_x == x, k == x % 2)
                block = gt.at[z // 2 - 1, k, y, source_x]

                @pl.when(stays)
                def _():
                    pltpu.make_async_copy(factor2.at[k], block, local.at[7]).wait()

                @pl.when(jnp.logical_not(stays))
                def _():
                    remote(
                        block, block, ga_send.at[0], ga_recv.at[source_x, x % 2], sibling
                    ).wait_recv()

    g_spread.landed(0)
    with scope("pass_coupling_x"):
        fxx.forward()
        gxx.forward()
    with scope("pass_panels_4"):
        passed_on(4)

    @pl.when(y != 0)
    def _():
        for distance in (2, 1, 3):
            xa_copy(distance).start()

    with scope("pass_first_factor"):
        f_gather.forward()
    with scope("finish_coupling_x"):
        fxx.finish()
        fx_to_sibling.start()
        gxx.finish()
        gx_to_sibling.start()
    with scope("finish_first_factor"):
        f_gather.finish()

    has_panel_rows = jnp.logical_and(y == 0, r < 8)
    with scope("turn_first_factor"):
        for panel in (0, 1):
            for part in range(4):
                high, rest = split(ft[panel, part].reshape(128, 384).T)
                at = (4 * panel + part) * 128
                wh[:, at : at + 128] = high
                wl[:, at : at + 128] = rest

        @pl.when(has_panel_rows)
        def _():
            row = lax.broadcasted_iota(jnp.int32, (128, 1024), 0)
            column = lax.broadcasted_iota(jnp.int32, (128, 1024), 1)
            unit = jnp.where(column == row + r * 128, -1.0, 0.0)
            wh[pl.ds(0, 128), :] = unit.astype(BF16)
            wl[pl.ds(0, 128), :] = jnp.zeros((128, 1024), BF16)

    with scope("wait_second_factor_1"):
        g_spread.landed(1)
        g_spread.landed(-1)
    with scope("wait_coupling_core"):
        load1.wait()
        fx_from_sibling.wait_recv()

    with scope("left_operator"):
        value1 = split(product((wh[:, 512:], wl[:, 512:]), split(i1[1])))
        vh[:, 512:], vl[:, 512:] = value1
        value0 = wh[:, :512].astype(F32) + wl[:, :512].astype(F32)
        for number in range(4):
            at = 512 + 128 * number
            value0 = value0 - product(
                (vh[:, at : at + 128], vl[:, at : at + 128]),
                split(fx[number % 2, number // 2].reshape(512, 128)),
                NT,
            )
        vh[:, :512], vl[:, :512] = split(product(split(value0), split(i1[0])))

    load2 = pltpu.make_async_copy(inverse2, i1, local.at[6])
    load2.start()
    with scope("wait_second_factor_2"):
        g_spread.landed(2)
        g_spread.landed(-2)
    with scope("finish_panels"):
        for event in EVENTS:
            arrived(event)

    def wait_slab(distance):
        remote(
            xt.at[y],
            xt.at[(y + 4 - distance) % 4],
            xa_send.at[distance - 1],
            xa_recv.at[distance - 1],
            sibling,
        ).wait_recv()

    def left(block):
        rows = split(xp[block].reshape(1024, 256))
        return xt[block] - product((vh[...], vl[...]), rows)

    def wait_panel_core(number, index):
        for source in range(4):
            xs_landing(number, index, source).wait_recv()

    with scope("wait_slab_0"):
        for distance in (1, 2, 3):

            @pl.when(y == distance)
            def _():
                wait_slab(distance)

        @pl.when(y == 0)
        def _():
            xa_own.wait()

    with scope("wait_panels_core"):
        @pl.when(in_panels(z))
        def _():
            own_panel().wait()

        for number, index in ((0, y), (1, (y + 3) % 4), (2, (y + 1) % 4), (3, (y + 2) % 4)):
            wait_panel_core(number, index)

    @pl.when(has_panel_rows)
    def _():
        xt[0, pl.ds(0, 128)] = jnp.zeros((128, 256), F32)

    with scope("left_update_0"):
        pb[x] = left(0)

    p_gather = Gather4(
        x,
        along_x,
        lambda index: pb.at[index],
        lambda part, index: pb.at[index, pl.ds(192 * part, 192)],
        p_send,
        p_recv,
    )
    p_gather.start()
    with scope("wait_right_operator"):
        load2.wait()
        gx_from_sibling.wait_recv()
    with scope("right_operator"):
        for panel in (0, 1):
            i2h[panel], i2l[panel] = split(i1[panel])
        total = None
        for part in (0, 1):
            at = 256 * part
            term = product(
                (i2h[1, :, at : at + 256], i2l[1, :, at : at + 256]),
                split(gx[part].reshape(512, 256)),
                NT,
            )
            total = term if total is None else total + term
        kh[...], kl[...] = split(product(split(total), (i2h[0], i2l[0])))

    with scope("wait_second_factor_3"):
        g_spread.landed(3)
        g_spread.landed(-3)
        g_spread.landed(4)
    g_gather.start()
    g_to_sibling(3, y).start()
    with scope("pass_columns"):
        p_gather.forward()
    with scope("wait_slab_rest"):
        for distance in (1, 2, 3):

            @pl.when(y != distance)
            def _():
                wait_slab(distance)

        @pl.when(y != 0)
        def _():
            xa_own.wait()

        @pl.when(has_panel_rows)
        def _():
            for block in range(1, 4):
                xt[block, pl.ds(0, 128)] = jnp.zeros((128, 256), F32)

    with scope("left_update_rest"):

        @pl.loop(1, 4)
        def _(block):
            db[block] = left(block)

    with scope("pass_second_factor"):
        g_gather.forward(then=lambda number, index: g_to_sibling(number, index).start())

    with scope("finish_columns"):
        p_gather.finish()

    with scope("solve_columns"):
        for half in (0, 1):
            rows = pl.ds(256 * half, 256)
            first = None
            second = None
            for part in range(2):
                at = 256 * part
                left0 = split(pb[part])
                left1 = split(pb[2 + part])
                term0 = product(left0, (i2h[0, rows, at : at + 256], i2l[0, rows, at : at + 256]), NT)
                term1 = product(
                    left1, (i2h[1, rows, at : at + 256], i2l[1, rows, at : at + 256]), NT
                ) - product(left0, (kh[rows, at : at + 256], kl[rows, at : at + 256]), NT)
                first = term0 if first is None else first + term0
                second = term1 if second is None else second + term1
            for number, value in ((half, first), (2 + half, second)):
                at = 256 * number
                zh[:, at : at + 256], zl[:, at : at + 256] = split(value)

                @pl.when(x == number)
                def _():
                    db[0] = value

    out_rows = out.at[pl.ds(pl.multiple_of(r * 96, 32), 96), :]

    def own_rows_of(block):
        return db.at[block, pl.ds(pl.multiple_of(96 * x, 32), 96)]

    def turn_x(block, distance):
        to = (x + distance) % 4
        return remote(
            db.at[block, pl.ds(pl.multiple_of(96 * to, 32), 96)],
            eb.at[x, block],
            e_send.at[block, distance - 1],
            e_recv.at[block, distance - 1],
            along_x(to),
        )

    def turn_z(block, distance, remote_do, local_do):
        from_x = (x + 4 - distance) % 4
        src = own_rows_of(block) if distance == 0 else eb.at[from_x, block]
        to = 4 * block + from_x

        @pl.when(to == r)
        def _():
            local_do(pltpu.make_async_copy(src, out_rows, local.at[8]))

        @pl.when(to != r)
        def _():
            remote_do(
                remote(src, out_rows, o_send.at[block, distance], o_recv.at[r], (to, c))
            )

    def start(copy):
        copy.start()

    with scope("finish_second_factor"):
        g_gather.finish(then=lambda number, index: g_to_sibling(number, index).start())
        for number, index in ((3, y), (0, g_gather.down), (1, g_gather.up), (2, g_gather.far)):
            g_from_sibling(number, index).wait_recv()
    with scope("right_update"):
        for turn in (2, 1, 3, 0):
            block = (z // 2 + turn) % 4

            @pl.when(block != 0)
            def _():
                factor = split(gt[block - 1].reshape(1024, 256))
                db[block] = db[block] - product((zh[...], zl[...]), factor)

            for distance in (2, 1, 3):
                turn_x(block, distance).start()
            turn_z(block, 0, start, start)
    with scope("pass_out"):
        for turn in (2, 1, 3, 0):
            block = (z // 2 + turn) % 4
            for distance in (1, 3, 2):
                here = eb.at[(x + 4 - distance) % 4, block]
                remote(
                    here,
                    here,
                    e_send.at[block, distance - 1],
                    e_recv.at[block, distance - 1],
                    sibling,
                ).wait_recv()
                turn_z(block, distance, start, start)

    with scope("wait_out"):
        for source in range(16):
            rows = out.at[pl.ds(96 * source, 96), :]

            @pl.when(source != r)
            def _():
                remote(rows, rows, o_send.at[0, 0], o_recv.at[source], sibling).wait_recv()

    with scope("drain"):
        for block in range(4):
            for distance in range(4):
                turn_z(block, distance, lambda copy: copy.wait_send(), lambda copy: copy.wait())
            for distance in (1, 2, 3):
                turn_x(block, distance).wait_send()
        for event in EVENTS:
            sent(event)
            g_spread.sent(event)

        @pl.when(f_source)
        def _():
            for distance in range(1, 8):
                fz_copy(distance).wait_send()

        @pl.when(z == 1)
        def _():
            for distance in range(1, 8):
                gz_copy(distance).wait_send()

        for distance in (1, 2, 3):
            fa_copy(distance).wait_send()
            xa_copy(distance).wait_send()
        for panel in (0, 1):

            @pl.when(jnp.logical_and(z >= 2, jnp.logical_not(ga_stays(panel))))
            def _():
                ga_copy(panel).wait_send()

        for gather in (fxx, fxy, gxx, gxy, f_gather, p_gather, g_gather):
            gather.drain()
        fx_to_sibling.wait_send()
        gx_to_sibling.wait_send()
        for number, index in ((3, y), (0, g_gather.down), (1, g_gather.up), (2, g_gather.far)):
            g_to_sibling(number, index).wait_send()


def on_device(*arrays):
    dma = pltpu.SemaphoreType.DMA
    any_space = pl.BlockSpec(memory_space=pl.ANY)
    scratch = [
        pltpu.VMEM((2, 512, 512), F32),
        pltpu.VMEM((2, 512, 512), BF16),
        pltpu.VMEM((2, 512, 512), BF16),
        pltpu.VMEM((512, 512), BF16),
        pltpu.VMEM((512, 512), BF16),
        pltpu.VMEM((4, 384, 256), F32),
        pltpu.VMEM((4, 8, 128, 256), F32),
        pltpu.VMEM((2, 2, 4, 4, 32, 128), F32),
        pltpu.VMEM((2, 4, 4, 32, 256), F32),
        pltpu.VMEM((2, 4, 4, 32, 384), F32),
        pltpu.VMEM((384, 1024), BF16),
        pltpu.VMEM((384, 1024), BF16),
        pltpu.VMEM((384, 1024), BF16),
        pltpu.VMEM((384, 1024), BF16),
        pltpu.VMEM((3, 2, 4, 4, 32, 256), F32),
        pltpu.VMEM((4, 384, 256), F32),
        pltpu.VMEM((384, 1024), BF16),
        pltpu.VMEM((384, 1024), BF16),
        pltpu.VMEM((4, 384, 256), F32),
        pltpu.VMEM((4, 4, 96, 256), F32),
        dma((9,)),
        dma((4,)),
        dma((4,)),
        dma((4,)),
        dma((4,)),
        dma((4, 4)),
        dma((4, 4)),
        dma((4, 4)),
        dma((4, 4)),
        dma((7,)),
        dma((2,)),
        dma((7,)),
        dma((1,)),
        dma((4,)),
        dma((4,)),
        dma((4,)),
        dma((4,)),
        dma((4,)),
        dma((4,)),
        dma((4,)),
        dma((4,)),
        dma((2,)),
        dma((2,)),
        dma((3,)),
        dma((3,)),
        dma((4,)),
        dma((4,)),
        dma((3,)),
        dma((3,)),
        dma((2,)),
        dma((4, 2)),
        dma((8,)),
        dma((8,)),
        dma((8,)),
        dma((8,)),
        dma((4,)),
        dma((4,)),
        dma((4,)),
        dma((4,)),
        dma((4,)),
        dma((4,)),
        dma((4, 3)),
        dma((4, 3)),
        dma((4, 4)),
        dma((16,)),
    ]
    return pl.pallas_call(
        kernel,
        out_shape=jax.ShapeDtypeStruct((1536, 256), F32),
        in_specs=[any_space] * 5,
        out_specs=any_space,
        scratch_shapes=scratch,
        compiler_params=pltpu.CompilerParams(
            has_side_effects=True, collective_id=0, vmem_limit_bytes=56 * 1024 * 1024
        ),
        name="two_sided_panels",
    )(*arrays)


def solution(mesh):
    return jax.shard_map(
        on_device,
        mesh=mesh,
        in_specs=(P("rows", "cols"), P(), P(None, "cols", "rows"), P(), P(None, "cols", "rows")),
        out_specs=P("cols", "rows"),
        check_vma=False,
    )
```

```python
import jax
import jax.numpy as jnp
from jax import lax
from jax.experimental import pallas as pl
from jax.experimental.pallas import tpu as pltpu
from jax.sharding import PartitionSpec as P

MESH = pl.DeviceIdType.MESH
F32 = jnp.float32
BF16 = jnp.bfloat16
NN = (((1,), (0,)), ((), ()))
NT = (((1,), (1,)), ((), ()))


def split(value):
    high = value.astype(BF16)
    return high, (value - high.astype(F32)).astype(BF16)


def product(a, b, dims=NN):
    def dot(u, v):
        return lax.dot_general(u, v, dims, preferred_element_type=F32)

    return dot(a[0], b[0]) + (dot(a[0], b[1]) + dot(a[1], b[0]))


def remote(src, dst, send_sem, recv_sem, device):
    return pltpu.make_async_remote_copy(
        src_ref=src,
        dst_ref=dst,
        send_sem=send_sem,
        recv_sem=recv_sem,
        device_id=device,
        device_id_type=MESH,
    )


class Gather4:
    def __init__(self, index, device, slot, half, send, recv, src=None):
        self.up, self.down, self.far = (index + 1) % 4, (index + 3) % 4, (index + 2) % 4
        self.slot = slot
        to_up, to_down = device(self.up), device(self.down)
        own = slot(index)
        self.first = [
            remote(own if src is None else src, own, send.at[0], recv.at[0], to_up),
            remote(own if src is None else src, own, send.at[1], recv.at[1], to_down),
        ]
        self.second = [
            remote(half(0, self.down), half(0, self.down), send.at[2], recv.at[2], to_up),
            remote(half(1, self.up), half(1, self.up), send.at[3], recv.at[3], to_down),
        ]
        self.landing = [
            remote(own, slot(self.down), send.at[0], recv.at[0], to_up),
            remote(own, slot(self.up), send.at[1], recv.at[1], to_down),
            remote(half(0, self.far), half(0, self.far), send.at[2], recv.at[2], to_up),
            remote(half(1, self.far), half(1, self.far), send.at[3], recv.at[3], to_down),
        ]

    def start(self):
        for copy in self.first:
            copy.start()

    def forward(self, then=None):
        for way in (0, 1):
            self.landing[way].wait_recv()
            self.second[way].start()
            if then is not None:
                then(way, (self.down, self.up)[way])

    def finish(self, then=None):
        self.landing[2].wait_recv()
        self.landing[3].wait_recv()
        if then is not None:
            then(2, self.far)

    def drain(self):
        for copy in self.first + self.second:
            copy.wait_send()


class Spread8:
    def __init__(self, z, device, is_source, block, up, down):
        self.z, self.is_source, self.block, self.up, self.down = z, is_source, block, up, down
        self.above, self.below = device((z + 1) % 8), device((z + 7) % 8)

    def source(self, event):
        return (self.z + 16 - event) % 8

    def copy(self, way, source, src=None):
        block = self.block(source)
        send, recv = self.up if way > 0 else self.down
        to = self.above if way > 0 else self.below
        return remote(
            block if src is None else src, block, send.at[source], recv.at[source], to
        )

    def landed(self, event, then=None, src=None):
        source = self.source(event)

        @pl.when(self.is_source(source))
        def _():
            if event != 0:
                self.copy(1 if event > 0 else -1, source).wait_recv()
            if 0 <= event < 4:
                self.copy(1, source, src).start()
            if -3 < event <= 0:
                self.copy(-1, source, src).start()
            if then is not None:
                then(source)

    def sent(self, event, then=None):
        source = self.source(event)

        @pl.when(self.is_source(source))
        def _():
            if 0 <= event < 4:
                self.copy(1, source).wait_send()
            if -3 < event <= 0:
                self.copy(-1, source).wait_send()
            if then is not None:
                then(source)


EVENTS = (0, 1, -1, 2, -2, 3, -3, 4)


class Flow:
    def __init__(self, z, y, k, is_source, key, block, half, devices, sems):
        self.z, self.y, self.k, self.is_source, self.key = z, y, k, is_source, key
        self.block, self.half = block, half
        self.along_y, self.sibling = devices[1], devices[2]
        self.up, self.down, self.over, self.core = sems
        self.spread = Spread8(
            z,
            devices[0],
            is_source,
            lambda source: block(y, source, k),
            self.up,
            self.down,
        )

    def indices(self):
        return self.y, (self.y + 3) % 4, (self.y + 1) % 4, (self.y + 2) % 4

    def gather(self, source, src=None):
        key = self.key(source)
        return Gather4(
            self.y,
            self.along_y,
            lambda index: self.block(index, source, self.k),
            lambda part, index: self.half(part, index, source),
            self.over[0].at[key],
            self.over[1].at[key],
            src,
        )

    def to_core(self, number, source, core, src=None):
        block = self.block(self.indices()[number], source, core)
        send, recv = self.core
        key = self.key(source)
        return remote(
            block if src is None else src,
            block,
            send.at[number, key],
            recv.at[number, key],
            self.sibling,
        )

    def landed(self, *events, src=None, over=True):
        def then(source):
            if over:
                self.gather(source, src).start()
            self.to_core(0, source, self.k, src).start()

        for event in events:
            self.spread.landed(event, then, src)

    def go_over(self, *events):
        for event in events:
            source = self.spread.source(event)

            @pl.when(self.is_source(source))
            def _():
                self.gather(source).start()

    def passed(self, *events):
        for event in events:
            source = self.spread.source(event)

            @pl.when(self.is_source(source))
            def _():
                self.gather(source).forward(
                    then=lambda number, index: self.to_core(1 + number, source, self.k).start()
                )

    def arrived(self, *events):
        for event in events:
            source = self.spread.source(event)

            @pl.when(self.is_source(source))
            def _():
                self.gather(source).finish(
                    then=lambda number, index: self.to_core(1 + number, source, self.k).start()
                )

    def wait_core(self, number, source):
        self.to_core(number, source, 1 - self.k).wait_recv()

    def sent(self):
        def then(source):
            self.gather(source).drain()
            for number in range(4):
                self.to_core(number, source, self.k).wait_send()

        for event in EVENTS:
            self.spread.sent(event, then)


def kernel(
    slab,
    inverse1,
    factor1,
    inverse2,
    factor2,
    out,
    i1,
    i2h,
    i2l,
    kh,
    kl,
    xt,
    xp,
    fx,
    gx,
    ft,
    wh,
    wl,
    vh,
    vl,
    gt,
    pb,
    zh,
    zl,
    db,
    eb,
    local,
    up_send,
    up_recv,
    down_send,
    down_recv,
    py_send,
    py_recv,
    xs_send,
    xs_recv,
    fz_send,
    fz_recv,
    gz_send,
    gz_recv,
    fxx_send,
    fxx_recv,
    fxy_send,
    fxy_recv,
    gxx_send,
    gxx_recv,
    gxy_send,
    gxy_recv,
    sib_send,
    sib_recv,
    fa_send,
    fa_recv,
    ft_send,
    ft_recv,
    xa_send,
    xa_recv,
    ga_send,
    ga_recv,
    gu_send,
    gu_recv,
    gd_send,
    gd_recv,
    gy_send,
    gy_recv,
    gs_send,
    gs_recv,
    p_send,
    p_recv,
    e_send,
    e_recv,
    o_send,
    o_recv,
):
    r = lax.axis_index("rows")
    c = lax.axis_index("cols")
    z, k = r // 2, r % 2
    y, x = c // 4, c % 4
    sibling = (2 * z + 1 - k, c)
    scope = jax.named_scope

    def along_y(index):
        return (r, 4 * index + x)

    def along_x(index):
        return (r, 4 * y + index)

    def along_z(index):
        return (2 * index + k, c)

    panel_rows = slab.at[pl.ds(0, 128), :]

    def in_panels(source):
        return source < 4

    panels = Flow(
        z,
        y,
        k,
        in_panels,
        lambda source: source,
        lambda index, source, core: xp.at[index, 2 * source + core],
        lambda part, index, source: xp.at[index, 2 * source + k, pl.ds(64 * part, 64)],
        (along_z, along_y, sibling),
        ((up_send, up_recv), (down_send, down_recv), (py_send, py_recv), (xs_send, xs_recv)),
    )

    def own_panel():
        return pltpu.make_async_copy(panel_rows, xp.at[y, 2 * z + k], local.at[0])

    with scope("barrier"):
        barrier = pltpu.get_barrier_semaphore()
        for distance in range(1, 4):
            over_x = (x + distance) % 4
            for device in (
                along_y((y + distance) % 4),
                along_x(over_x),
                (2 * z + 1 - k, 4 * y + over_x),
            ):
                pl.semaphore_signal(barrier, inc=1, device_id=device, device_id_type=MESH)
        for distance in range(1, 16):
            pl.semaphore_signal(
                barrier, inc=1, device_id=((r + distance) % 16, c), device_id_type=MESH
            )
        pl.semaphore_wait(barrier, 24)

    panels.landed(0, src=panel_rows)

    @pl.when(in_panels(z))
    def _():
        own_panel().start()

    fz_src = factor1.at[0, :, pl.ds(0, 128)]
    gz_src = factor2.at[0]

    def fz_dst(which):
        return fx.at[k, which, y, x]

    gz_dst = gx.at[k, y, x]
    fz_own = pltpu.make_async_copy(fz_src, fz_dst(z % 2), local.at[1])
    gz_own = pltpu.make_async_copy(gz_src, gz_dst, local.at[2])
    f_source = jnp.logical_or(z == 2, z == 3)

    def fz_copy(distance):
        return remote(
            fz_src,
            fz_dst(z % 2),
            fz_send.at[distance - 1],
            fz_recv.at[z % 2],
            along_z((z + distance) % 8),
        )

    def gz_copy(distance):
        return remote(
            gz_src, gz_dst, gz_send.at[distance - 1], gz_recv.at[0], along_z((z + distance) % 8)
        )

    @pl.when(f_source)
    def _():
        fz_own.start()
        for distance in range(1, 8):
            fz_copy(distance).start()

    def fa_copy(distance):
        to = (y + distance) % 4
        columns = pl.ds(pl.multiple_of(to * 384, 128), 384)
        return remote(
            factor1.at[:, :, columns],
            ft.at[:, y, x],
            fa_send.at[distance - 1],
            fa_recv.at[distance - 1],
            along_y(to),
        )

    fa_own = pltpu.make_async_copy(
        factor1.at[:, :, pl.ds(pl.multiple_of(y * 384, 128), 384)], ft.at[:, y, x], local.at[3]
    )
    fa_own.start()
    for distance in (2, 1, 3):
        fa_copy(distance).start()

    load1 = pltpu.make_async_copy(inverse1, i1, local.at[5])
    load1.start()

    @pl.when(z == 1)
    def _():
        gz_own.start()
        for distance in range(1, 8):
            gz_copy(distance).start()

    g_plane = r % 4
    g_block = r // 4

    def ga_copy(panel):
        return remote(
            factor2.at[panel],
            gt.at[g_block - 1, panel, y, x],
            ga_send.at[panel],
            ga_recv.at[x, k],
            (2 * z + panel, 4 * y + g_plane),
        )

    def ga_own(panel):
        return pltpu.make_async_copy(
            factor2.at[panel], gt.at[g_block - 1, panel, y, x], local.at[7]
        )

    def ga_stays(panel):
        return jnp.logical_and(g_plane == x, k == panel)

    for panel in (0, 1):

        @pl.when(jnp.logical_and(z >= 2, ga_stays(panel)))
        def _():
            ga_own(panel).start()

        @pl.when(jnp.logical_and(z >= 2, jnp.logical_not(ga_stays(panel))))
        def _():
            ga_copy(panel).start()

    def g_source(source):
        return jnp.logical_and(source >= 2, source % 2 == x // 2)

    seconds = Flow(
        z,
        y,
        k,
        g_source,
        lambda source: source // 2 - 1,
        lambda index, source, core: gt.at[source // 2 - 1, core, index],
        lambda part, index, source: gt.at[source // 2 - 1, k, index, pl.ds(2 * part, 2)],
        (along_z, along_y, sibling),
        ((gu_send, gu_recv), (gd_send, gd_recv), (gy_send, gy_recv), (gs_send, gs_recv)),
    )

    def xa_copy(distance):
        to = (y + distance) % 4
        return remote(
            slab.at[pl.ds(pl.multiple_of(to * 384, 128), 384), :],
            xt.at[y],
            xa_send.at[distance - 1],
            xa_recv.at[distance - 1],
            along_y(to),
        )

    xa_own = pltpu.make_async_copy(
        slab.at[pl.ds(pl.multiple_of(y * 384, 128), 384), :], xt.at[y], local.at[4]
    )

    fxy = Gather4(
        y,
        along_y,
        lambda index: fx.at[k, :, index, x],
        lambda part, index: fx.at[k, part, index, x],
        fxy_send,
        fxy_recv,
    )
    fxx = Gather4(
        x,
        along_x,
        lambda index: fx.at[k, :, :, index],
        lambda part, index: fx.at[k, part, :, index],
        fxx_send,
        fxx_recv,
    )
    gxy = Gather4(
        y,
        along_y,
        lambda index: gx.at[k, index, x],
        lambda part, index: gx.at[k, index, x, pl.ds(16 * part, 16)],
        gxy_send,
        gxy_recv,
    )
    gxx = Gather4(
        x,
        along_x,
        lambda index: gx.at[k, :, index],
        lambda part, index: gx.at[k, pl.ds(2 * part, 2), index],
        gxx_send,
        gxx_recv,
    )
    f_gather = Gather4(
        x,
        along_x,
        lambda index: ft.at[:, :, index],
        lambda part, index: ft.at[part, :, index],
        ft_send,
        ft_recv,
    )
    fx_to_sibling = remote(fx.at[k], fx.at[k], sib_send.at[0], sib_recv.at[0], sibling)
    gx_to_sibling = remote(gx.at[k], gx.at[k], sib_send.at[1], sib_recv.at[1], sibling)
    fx_from_sibling = remote(fx.at[1 - k], fx.at[1 - k], sib_send.at[0], sib_recv.at[0], sibling)
    gx_from_sibling = remote(gx.at[1 - k], gx.at[1 - k], sib_send.at[1], sib_recv.at[1], sibling)

    with scope("panels_1"):
        panels.landed(1, -1)
        panels.passed(0)
    with scope("first_factor_y"):
        fa_own.wait()
        for distance in (1, 3, 2):
            remote(
                ft.at[:, y, x],
                ft.at[:, (y + 4 - distance) % 4, x],
                fa_send.at[distance - 1],
                fa_recv.at[distance - 1],
                sibling,
            ).wait_recv()
    f_gather.start()
    with scope("coupling_z"):
        for which in (0, 1):

            @pl.when(z == 2 + which)
            def _():
                fz_own.wait()

            @pl.when(z != 2 + which)
            def _():
                remote(
                    fz_src, fz_dst(which), fz_send.at[0], fz_recv.at[which], sibling
                ).wait_recv()

    fxy.start()
    with scope("second_coupling_z"):

        @pl.when(z == 1)
        def _():
            gz_own.wait()

        @pl.when(z != 1)
        def _():
            remote(gz_src, gz_dst, gz_send.at[0], gz_recv.at[0], sibling).wait_recv()

    gxy.start()
    with scope("panels_2"):
        panels.landed(2, -2)
        panels.passed(1, -1)
    with scope("pass_coupling_y"):
        fxy.forward()
        gxy.forward()
    with scope("panels_3"):
        panels.landed(3, -3)
        panels.passed(2, -2)
    with scope("finish_coupling_y"):
        fxy.finish()
    fxx.start()
    with scope("pass_first_factor"):
        f_gather.forward()
    with scope("panels_4"):
        panels.landed(4)
        panels.passed(3, -3)
    with scope("finish_second_coupling_y"):
        gxy.finish()
    gxx.start()
    with scope("pass_coupling_x"):
        fxx.forward()
    with scope("second_factor_x"):

        @pl.when(g_source(z))
        def _():
            for source_x in range(4):
                stays = jnp.logical_and(source_x == x, k == x % 2)
                block = gt.at[z // 2 - 1, k, y, source_x]

                @pl.when(stays)
                def _():
                    pltpu.make_async_copy(factor2.at[k], block, local.at[7]).wait()

                @pl.when(jnp.logical_not(stays))
                def _():
                    remote(
                        block, block, ga_send.at[0], ga_recv.at[source_x, x % 2], sibling
                    ).wait_recv()

    seconds.landed(0, over=False)
    with scope("pass_panels_4"):
        panels.passed(4)
    xa_own.start()

    @pl.when(y == 0)
    def _():
        for distance in (2, 1, 3):
            xa_copy(distance).start()

    @pl.when(y != 0)
    def _():
        for distance in (2, 1, 3):
            xa_copy(distance).start()

    with scope("finish_first_factor"):
        f_gather.finish()

    has_panel_rows = jnp.logical_and(y == 0, r < 8)
    with scope("turn_first_factor"):
        for panel in (0, 1):
            for part in range(4):
                high, rest = split(ft[panel, part].reshape(128, 384).T)
                at = (4 * panel + part) * 128
                wh[:, at : at + 128] = high
                wl[:, at : at + 128] = rest

        @pl.when(has_panel_rows)
        def _():
            row = lax.broadcasted_iota(jnp.int32, (128, 1024), 0)
            column = lax.broadcasted_iota(jnp.int32, (128, 1024), 1)
            unit = jnp.where(column == row + r * 128, -1.0, 0.0)
            wh[pl.ds(0, 128), :] = unit.astype(BF16)
            wl[pl.ds(0, 128), :] = jnp.zeros((128, 1024), BF16)

    with scope("finish_coupling_x"):
        fxx.finish()
    fx_to_sibling.start()
    with scope("pass_second_coupling_x"):
        gxx.forward()
    with scope("seconds_1"):
        seconds.landed(1, -1, over=False)
    with scope("arrived_panels_1"):
        panels.arrived(0, 1, -1)
    with scope("coupling_core"):
        load1.wait()
        fx_from_sibling.wait_recv()

    with scope("left_operator"):
        value1 = split(product((wh[:, 512:], wl[:, 512:]), split(i1[1])))
        vh[:, 512:], vl[:, 512:] = value1
        value0 = wh[:, :512].astype(F32) + wl[:, :512].astype(F32)
        for number in range(4):
            at = 512 + 128 * number
            value0 = value0 - product(
                (vh[:, at : at + 128], vl[:, at : at + 128]),
                split(fx[number % 2, number // 2].reshape(512, 128)),
                NT,
            )
        vh[:, :512], vl[:, :512] = split(product(split(value0), split(i1[0])))

    load2 = pltpu.make_async_copy(inverse2, i1, local.at[6])
    load2.start()
    with scope("finish_second_coupling_x"):
        gxx.finish()
    gx_to_sibling.start()
    with scope("arrived_panels_2"):
        panels.arrived(2, -2, 3, -3, 4)
    with scope("seconds_2"):
        seconds.landed(2, -2, over=False)
    seconds.go_over(0, 1, -1, 2, -2)

    def wait_slab(distance):
        remote(
            xt.at[y],
            xt.at[(y + 4 - distance) % 4],
            xa_send.at[distance - 1],
            xa_recv.at[distance - 1],
            sibling,
        ).wait_recv()

    def left(block):
        rows = split(xp[block].reshape(1024, 256))
        return xt[block] - product((vh[...], vl[...]), rows)

    with scope("wait_slab_0"):
        for distance in (1, 2, 3):

            @pl.when(y == distance)
            def _():
                wait_slab(distance)

        @pl.when(y == 0)
        def _():
            xa_own.wait()

    with scope("wait_panels_core"):
        @pl.when(in_panels(z))
        def _():
            own_panel().wait()

        for number in range(4):
            for source in range(4):
                panels.wait_core(number, source)

    @pl.when(has_panel_rows)
    def _():
        xt[0, pl.ds(0, 128)] = jnp.zeros((128, 256), F32)

    with scope("left_update_0"):
        pb[x] = left(0)

    p_gather = Gather4(
        x,
        along_x,
        lambda index: pb.at[index],
        lambda part, index: pb.at[index, pl.ds(192 * part, 192)],
        p_send,
        p_recv,
    )
    p_gather.start()
    with scope("seconds_3"):
        seconds.landed(3, -3)
    with scope("wait_right_operator"):
        load2.wait()
        gx_from_sibling.wait_recv()
    with scope("right_operator"):
        for panel in (0, 1):
            i2h[panel], i2l[panel] = split(i1[panel])
        total = None
        for part in (0, 1):
            at = 256 * part
            term = product(
                (i2h[1, :, at : at + 256], i2l[1, :, at : at + 256]),
                split(gx[part].reshape(512, 256)),
                NT,
            )
            total = term if total is None else total + term
        kh[...], kl[...] = split(product(split(total), (i2h[0], i2l[0])))

    with scope("seconds_4"):
        seconds.landed(4)
    with scope("pass_columns"):
        p_gather.forward()
    with scope("wait_slab_rest"):
        for distance in (1, 2, 3):

            @pl.when(y != distance)
            def _():
                wait_slab(distance)

        @pl.when(y != 0)
        def _():
            xa_own.wait()

        @pl.when(has_panel_rows)
        def _():
            for block in range(1, 4):
                xt[block, pl.ds(0, 128)] = jnp.zeros((128, 256), F32)

    with scope("left_update_rest"):

        @pl.loop(1, 4)
        def _(block):
            db[block] = left(block)

    with scope("pass_seconds"):
        seconds.passed(*EVENTS)
    with scope("arrived_seconds"):
        seconds.arrived(*EVENTS)
    with scope("finish_columns"):
        p_gather.finish()

    with scope("solve_columns"):
        for half in (0, 1):
            rows = pl.ds(256 * half, 256)
            first = None
            second = None
            for part in range(2):
                at = 256 * part
                left0 = split(pb[part])
                left1 = split(pb[2 + part])
                term0 = product(left0, (i2h[0, rows, at : at + 256], i2l[0, rows, at : at + 256]), NT)
                term1 = product(
                    left1, (i2h[1, rows, at : at + 256], i2l[1, rows, at : at + 256]), NT
                ) - product(left0, (kh[rows, at : at + 256], kl[rows, at : at + 256]), NT)
                first = term0 if first is None else first + term0
                second = term1 if second is None else second + term1
            for number, value in ((half, first), (2 + half, second)):
                at = 256 * number
                zh[:, at : at + 256], zl[:, at : at + 256] = split(value)

                @pl.when(x == number)
                def _():
                    db[0] = value

    out_rows = out.at[pl.ds(pl.multiple_of(r * 96, 32), 96), :]

    def own_rows_of(block):
        return db.at[block, pl.ds(pl.multiple_of(96 * x, 32), 96)]

    def turn_x(block, distance):
        to = (x + distance) % 4
        return remote(
            db.at[block, pl.ds(pl.multiple_of(96 * to, 32), 96)],
            eb.at[x, block],
            e_send.at[block, distance - 1],
            e_recv.at[block, distance - 1],
            along_x(to),
        )

    def turn_z(block, distance, remote_do, local_do):
        from_x = (x + 4 - distance) % 4
        src = own_rows_of(block) if distance == 0 else eb.at[from_x, block]
        to = 4 * block + from_x

        @pl.when(to == r)
        def _():
            local_do(pltpu.make_async_copy(src, out_rows, local.at[8]))

        @pl.when(to != r)
        def _():
            remote_do(
                remote(src, out_rows, o_send.at[block, distance], o_recv.at[r], (to, c))
            )

    def start(copy):
        copy.start()

    with scope("seconds_core"):
        for number in range(4):
            for block in range(3):
                seconds.wait_core(number, 2 * block + 2)
    with scope("right_update"):
        for turn in (2, 1, 3, 0):
            block = (z // 2 + turn) % 4

            @pl.when(block != 0)
            def _():
                factor = split(gt[block - 1].reshape(1024, 256))
                db[block] = db[block] - product((zh[...], zl[...]), factor)

            for distance in (2, 1, 3):
                turn_x(block, distance).start()
            turn_z(block, 0, start, start)
    with scope("pass_out"):
        for turn in (2, 1, 3, 0):
            block = (z // 2 + turn) % 4
            for distance in (1, 3, 2):
                here = eb.at[(x + 4 - distance) % 4, block]
                remote(
                    here,
                    here,
                    e_send.at[block, distance - 1],
                    e_recv.at[block, distance - 1],
                    sibling,
                ).wait_recv()
                turn_z(block, distance, start, start)

    with scope("wait_out"):
        for source in range(16):
            rows = out.at[pl.ds(96 * source, 96), :]

            @pl.when(source != r)
            def _():
                remote(rows, rows, o_send.at[0, 0], o_recv.at[source], sibling).wait_recv()

    with scope("drain"):
        for block in range(4):
            for distance in range(4):
                turn_z(block, distance, lambda copy: copy.wait_send(), lambda copy: copy.wait())
            for distance in (1, 2, 3):
                turn_x(block, distance).wait_send()
        panels.sent()
        seconds.sent()

        @pl.when(f_source)
        def _():
            for distance in range(1, 8):
                fz_copy(distance).wait_send()

        @pl.when(z == 1)
        def _():
            for distance in range(1, 8):
                gz_copy(distance).wait_send()

        for distance in (1, 2, 3):
            fa_copy(distance).wait_send()
            xa_copy(distance).wait_send()
        for panel in (0, 1):

            @pl.when(jnp.logical_and(z >= 2, jnp.logical_not(ga_stays(panel))))
            def _():
                ga_copy(panel).wait_send()

        for gather in (fxx, fxy, gxx, gxy, f_gather, p_gather):
            gather.drain()
        fx_to_sibling.wait_send()
        gx_to_sibling.wait_send()


def on_device(*arrays):
    dma = pltpu.SemaphoreType.DMA
    any_space = pl.BlockSpec(memory_space=pl.ANY)
    scratch = [
        pltpu.VMEM((2, 512, 512), F32),
        pltpu.VMEM((2, 512, 512), BF16),
        pltpu.VMEM((2, 512, 512), BF16),
        pltpu.VMEM((512, 512), BF16),
        pltpu.VMEM((512, 512), BF16),
        pltpu.VMEM((4, 384, 256), F32),
        pltpu.VMEM((4, 8, 128, 256), F32),
        pltpu.VMEM((2, 2, 4, 4, 32, 128), F32),
        pltpu.VMEM((2, 4, 4, 32, 256), F32),
        pltpu.VMEM((2, 4, 4, 32, 384), F32),
        pltpu.VMEM((384, 1024), BF16),
        pltpu.VMEM((384, 1024), BF16),
        pltpu.VMEM((384, 1024), BF16),
        pltpu.VMEM((384, 1024), BF16),
        pltpu.VMEM((3, 2, 4, 4, 32, 256), F32),
        pltpu.VMEM((4, 384, 256), F32),
        pltpu.VMEM((384, 1024), BF16),
        pltpu.VMEM((384, 1024), BF16),
        pltpu.VMEM((4, 384, 256), F32),
        pltpu.VMEM((4, 4, 96, 256), F32),
        dma((9,)),
        dma((4,)),
        dma((4,)),
        dma((4,)),
        dma((4,)),
        dma((4, 4)),
        dma((4, 4)),
        dma((4, 4)),
        dma((4, 4)),
        dma((7,)),
        dma((2,)),
        dma((7,)),
        dma((1,)),
        dma((4,)),
        dma((4,)),
        dma((4,)),
        dma((4,)),
        dma((4,)),
        dma((4,)),
        dma((4,)),
        dma((4,)),
        dma((2,)),
        dma((2,)),
        dma((3,)),
        dma((3,)),
        dma((4,)),
        dma((4,)),
        dma((3,)),
        dma((3,)),
        dma((2,)),
        dma((4, 2)),
        dma((8,)),
        dma((8,)),
        dma((8,)),
        dma((8,)),
        dma((3, 4)),
        dma((3, 4)),
        dma((4, 3)),
        dma((4, 3)),
        dma((4,)),
        dma((4,)),
        dma((4, 3)),
        dma((4, 3)),
        dma((4, 4)),
        dma((16,)),
    ]
    return pl.pallas_call(
        kernel,
        out_shape=jax.ShapeDtypeStruct((1536, 256), F32),
        in_specs=[any_space] * 5,
        out_specs=any_space,
        scratch_shapes=scratch,
        compiler_params=pltpu.CompilerParams(
            has_side_effects=True, collective_id=0, vmem_limit_bytes=56 * 1024 * 1024
        ),
        name="two_sided_panels",
    )(*arrays)


def solution(mesh):
    return jax.shard_map(
        on_device,
        mesh=mesh,
        in_specs=(P("rows", "cols"), P(), P(None, "cols", "rows"), P(), P(None, "cols", "rows")),
        out_specs=P("cols", "rows"),
        check_vma=False,
    )
```

```python
import jax
import jax.numpy as jnp
from jax import lax
from jax.experimental import pallas as pl
from jax.experimental.pallas import tpu as pltpu
from jax.sharding import PartitionSpec as P

MESH = pl.DeviceIdType.MESH
F32 = jnp.float32
BF16 = jnp.bfloat16
NN = (((1,), (0,)), ((), ()))
NT = (((1,), (1,)), ((), ()))


def split(value):
    high = value.astype(BF16)
    return high, (value - high.astype(F32)).astype(BF16)


def product(a, b, dims=NN):
    def dot(u, v):
        return lax.dot_general(u, v, dims, preferred_element_type=F32)

    return dot(a[0], b[0]) + (dot(a[0], b[1]) + dot(a[1], b[0]))


def remote(src, dst, send_sem, recv_sem, device):
    return pltpu.make_async_remote_copy(
        src_ref=src,
        dst_ref=dst,
        send_sem=send_sem,
        recv_sem=recv_sem,
        device_id=device,
        device_id_type=MESH,
    )


class Gather4:
    def __init__(self, index, device, slot, half, send, recv, src=None):
        self.up, self.down, self.far = (index + 1) % 4, (index + 3) % 4, (index + 2) % 4
        self.slot = slot
        to_up, to_down = device(self.up), device(self.down)
        own = slot(index)
        self.first = [
            remote(own if src is None else src, own, send.at[0], recv.at[0], to_up),
            remote(own if src is None else src, own, send.at[1], recv.at[1], to_down),
        ]
        self.second = [
            remote(half(0, self.down), half(0, self.down), send.at[2], recv.at[2], to_up),
            remote(half(1, self.up), half(1, self.up), send.at[3], recv.at[3], to_down),
        ]
        self.landing = [
            remote(own, slot(self.down), send.at[0], recv.at[0], to_up),
            remote(own, slot(self.up), send.at[1], recv.at[1], to_down),
            remote(half(0, self.far), half(0, self.far), send.at[2], recv.at[2], to_up),
            remote(half(1, self.far), half(1, self.far), send.at[3], recv.at[3], to_down),
        ]

    def start(self):
        for copy in self.first:
            copy.start()

    def forward(self, then=None):
        for way in (0, 1):
            self.landing[way].wait_recv()
            self.second[way].start()
            if then is not None:
                then(way, (self.down, self.up)[way])

    def finish(self, then=None):
        self.landing[2].wait_recv()
        self.landing[3].wait_recv()
        if then is not None:
            then(2, self.far)

    def drain(self):
        for copy in self.first + self.second:
            copy.wait_send()


class Spread8:
    def __init__(self, z, device, is_source, block, up, down):
        self.z, self.is_source, self.block, self.up, self.down = z, is_source, block, up, down
        self.above, self.below = device((z + 1) % 8), device((z + 7) % 8)

    def source(self, event):
        return (self.z + 16 - event) % 8

    def copy(self, way, source, src=None):
        block = self.block(source)
        send, recv = self.up if way > 0 else self.down
        to = self.above if way > 0 else self.below
        return remote(
            block if src is None else src, block, send.at[source], recv.at[source], to
        )

    def landed(self, event, then=None, src=None):
        source = self.source(event)

        @pl.when(self.is_source(source))
        def _():
            if event != 0:
                self.copy(1 if event > 0 else -1, source).wait_recv()
            if 0 <= event < 4:
                self.copy(1, source, src).start()
            if -3 < event <= 0:
                self.copy(-1, source, src).start()
            if then is not None:
                then(source)

    def sent(self, event, then=None):
        source = self.source(event)

        @pl.when(self.is_source(source))
        def _():
            if 0 <= event < 4:
                self.copy(1, source).wait_send()
            if -3 < event <= 0:
                self.copy(-1, source).wait_send()
            if then is not None:
                then(source)


EVENTS = (0, 1, -1, 2, -2, 3, -3, 4)


class Flow:
    def __init__(self, z, y, k, is_source, key, block, half, devices, sems):
        self.z, self.y, self.k, self.is_source, self.key = z, y, k, is_source, key
        self.block, self.half = block, half
        self.along_y, self.sibling = devices[1], devices[2]
        self.up, self.down, self.over, self.core = sems
        self.spread = Spread8(
            z,
            devices[0],
            is_source,
            lambda source: block(y, source, k),
            self.up,
            self.down,
        )

    def indices(self):
        return self.y, (self.y + 3) % 4, (self.y + 1) % 4, (self.y + 2) % 4

    def gather(self, source, src=None):
        key = self.key(source)
        return Gather4(
            self.y,
            self.along_y,
            lambda index: self.block(index, source, self.k),
            lambda part, index: self.half(part, index, source),
            self.over[0].at[key],
            self.over[1].at[key],
            src,
        )

    def to_core(self, number, source, core, src=None):
        block = self.block(self.indices()[number], source, core)
        send, recv = self.core
        key = self.key(source)
        return remote(
            block if src is None else src,
            block,
            send.at[number, key],
            recv.at[number, key],
            self.sibling,
        )

    def landed(self, *events, src=None, over=True):
        def then(source):
            if over:
                self.gather(source, src).start()
            self.to_core(0, source, self.k, src).start()

        for event in events:
            self.spread.landed(event, then, src)

    def go_over(self, *events):
        for event in events:
            source = self.spread.source(event)

            @pl.when(self.is_source(source))
            def _():
                self.gather(source).start()

    def passed(self, *events):
        for event in events:
            source = self.spread.source(event)

            @pl.when(self.is_source(source))
            def _():
                self.gather(source).forward(
                    then=lambda number, index: self.to_core(1 + number, source, self.k).start()
                )

    def arrived(self, *events):
        for event in events:
            source = self.spread.source(event)

            @pl.when(self.is_source(source))
            def _():
                self.gather(source).finish(
                    then=lambda number, index: self.to_core(1 + number, source, self.k).start()
                )

    def wait_core(self, number, source):
        self.to_core(number, source, 1 - self.k).wait_recv()

    def sent(self):
        def then(source):
            self.gather(source).drain()
            for number in range(4):
                self.to_core(number, source, self.k).wait_send()

        for event in EVENTS:
            self.spread.sent(event, then)


def kernel(
    slab,
    inverse1,
    factor1,
    inverse2,
    factor2,
    out,
    i1,
    i2h,
    i2l,
    kh,
    kl,
    xt,
    xp,
    fx,
    gx,
    ft,
    wh,
    wl,
    vh,
    vl,
    gt,
    pb,
    zh,
    zl,
    db,
    eb,
    local,
    up_send,
    up_recv,
    down_send,
    down_recv,
    py_send,
    py_recv,
    xs_send,
    xs_recv,
    fz_send,
    fz_recv,
    gz_send,
    gz_recv,
    fxx_send,
    fxx_recv,
    fxy_send,
    fxy_recv,
    gxx_send,
    gxx_recv,
    gxy_send,
    gxy_recv,
    sib_send,
    sib_recv,
    fa_send,
    fa_recv,
    ft_send,
    ft_recv,
    xa_send,
    xa_recv,
    ga_send,
    ga_recv,
    gu_send,
    gu_recv,
    gd_send,
    gd_recv,
    gy_send,
    gy_recv,
    gs_send,
    gs_recv,
    p_send,
    p_recv,
    e_send,
    e_recv,
    o_send,
    o_recv,
):
    r = lax.axis_index("rows")
    c = lax.axis_index("cols")
    z, k = r // 2, r % 2
    y, x = c // 4, c % 4
    sibling = (2 * z + 1 - k, c)
    scope = jax.named_scope

    def along_y(index):
        return (r, 4 * index + x)

    def along_x(index):
        return (r, 4 * y + index)

    def along_z(index):
        return (2 * index + k, c)

    panel_rows = slab.at[pl.ds(0, 128), :]

    def in_panels(source):
        return source < 4

    panels = Flow(
        z,
        y,
        k,
        in_panels,
        lambda source: source,
        lambda index, source, core: xp.at[index, 2 * source + core],
        lambda part, index, source: xp.at[index, 2 * source + k, pl.ds(64 * part, 64)],
        (along_z, along_y, sibling),
        ((up_send, up_recv), (down_send, down_recv), (py_send, py_recv), (xs_send, xs_recv)),
    )

    def own_panel():
        return pltpu.make_async_copy(panel_rows, xp.at[y, 2 * z + k], local.at[0])

    with scope("barrier"):
        barrier = pltpu.get_barrier_semaphore()
        for distance in range(1, 4):
            over_x = (x + distance) % 4
            for device in (
                along_y((y + distance) % 4),
                along_x(over_x),
                (2 * z + 1 - k, 4 * y + over_x),
            ):
                pl.semaphore_signal(barrier, inc=1, device_id=device, device_id_type=MESH)
        for distance in range(1, 16):
            pl.semaphore_signal(
                barrier, inc=1, device_id=((r + distance) % 16, c), device_id_type=MESH
            )
        pl.semaphore_wait(barrier, 24)

    panels.landed(0, src=panel_rows)

    @pl.when(in_panels(z))
    def _():
        own_panel().start()

    fz_src = factor1.at[0, :, pl.ds(0, 128)]
    gz_src = factor2.at[0]

    def fz_dst(which):
        return fx.at[k, which, y, x]

    gz_dst = gx.at[k, y, x]
    fz_own = pltpu.make_async_copy(fz_src, fz_dst(z % 2), local.at[1])
    gz_own = pltpu.make_async_copy(gz_src, gz_dst, local.at[2])
    f_source = jnp.logical_or(z == 2, z == 3)

    def fz_copy(distance):
        return remote(
            fz_src,
            fz_dst(z % 2),
            fz_send.at[distance - 1],
            fz_recv.at[z % 2],
            along_z((z + distance) % 8),
        )

    def gz_copy(distance):
        return remote(
            gz_src, gz_dst, gz_send.at[distance - 1], gz_recv.at[0], along_z((z + distance) % 8)
        )

    @pl.when(f_source)
    def _():
        fz_own.start()
        for distance in range(1, 8):
            fz_copy(distance).start()

    def fa_copy(distance):
        to = (y + distance) % 4
        columns = pl.ds(pl.multiple_of(to * 384, 128), 384)
        return remote(
            factor1.at[:, :, columns],
            ft.at[:, y, x],
            fa_send.at[distance - 1],
            fa_recv.at[distance - 1],
            along_y(to),
        )

    fa_own = pltpu.make_async_copy(
        factor1.at[:, :, pl.ds(pl.multiple_of(y * 384, 128), 384)], ft.at[:, y, x], local.at[3]
    )
    fa_own.start()
    for distance in (2, 1, 3):
        fa_copy(distance).start()

    load1 = pltpu.make_async_copy(inverse1, i1, local.at[5])
    load1.start()

    @pl.when(z == 1)
    def _():
        gz_own.start()
        for distance in range(1, 8):
            gz_copy(distance).start()

    g_plane = r % 4
    g_block = r // 4

    def ga_copy(panel):
        return remote(
            factor2.at[panel],
            gt.at[g_block - 1, panel, y, x],
            ga_send.at[panel],
            ga_recv.at[x, k],
            (2 * z + panel, 4 * y + g_plane),
        )

    def ga_own(panel):
        return pltpu.make_async_copy(
            factor2.at[panel], gt.at[g_block - 1, panel, y, x], local.at[7]
        )

    def ga_stays(panel):
        return jnp.logical_and(g_plane == x, k == panel)

    for panel in (0, 1):

        @pl.when(jnp.logical_and(z >= 2, ga_stays(panel)))
        def _():
            ga_own(panel).start()

        @pl.when(jnp.logical_and(z >= 2, jnp.logical_not(ga_stays(panel))))
        def _():
            ga_copy(panel).start()

    def g_source(source):
        return jnp.logical_and(source >= 2, source % 2 == x // 2)

    seconds = Flow(
        z,
        y,
        k,
        g_source,
        lambda source: source // 2 - 1,
        lambda index, source, core: gt.at[source // 2 - 1, core, index],
        lambda part, index, source: gt.at[source // 2 - 1, k, index, pl.ds(2 * part, 2)],
        (along_z, along_y, sibling),
        ((gu_send, gu_recv), (gd_send, gd_recv), (gy_send, gy_recv), (gs_send, gs_recv)),
    )

    def xa_copy(distance):
        to = (y + distance) % 4
        return remote(
            slab.at[pl.ds(pl.multiple_of(to * 384, 128), 384), :],
            xt.at[y],
            xa_send.at[distance - 1],
            xa_recv.at[distance - 1],
            along_y(to),
        )

    xa_own = pltpu.make_async_copy(
        slab.at[pl.ds(pl.multiple_of(y * 384, 128), 384), :], xt.at[y], local.at[4]
    )

    fxy = Gather4(
        y,
        along_y,
        lambda index: fx.at[k, :, index, x],
        lambda part, index: fx.at[k, part, index, x],
        fxy_send,
        fxy_recv,
    )
    fxx = Gather4(
        x,
        along_x,
        lambda index: fx.at[k, :, :, index],
        lambda part, index: fx.at[k, part, :, index],
        fxx_send,
        fxx_recv,
    )
    gxy = Gather4(
        y,
        along_y,
        lambda index: gx.at[k, index, x],
        lambda part, index: gx.at[k, index, x, pl.ds(16 * part, 16)],
        gxy_send,
        gxy_recv,
    )
    gxx = Gather4(
        x,
        along_x,
        lambda index: gx.at[k, :, index],
        lambda part, index: gx.at[k, pl.ds(2 * part, 2), index],
        gxx_send,
        gxx_recv,
    )
    f_gather = Gather4(
        x,
        along_x,
        lambda index: ft.at[:, :, index],
        lambda part, index: ft.at[part, :, index],
        ft_send,
        ft_recv,
    )
    fx_to_sibling = remote(fx.at[k], fx.at[k], sib_send.at[0], sib_recv.at[0], sibling)
    gx_to_sibling = remote(gx.at[k], gx.at[k], sib_send.at[1], sib_recv.at[1], sibling)
    fx_from_sibling = remote(fx.at[1 - k], fx.at[1 - k], sib_send.at[0], sib_recv.at[0], sibling)
    gx_from_sibling = remote(gx.at[1 - k], gx.at[1 - k], sib_send.at[1], sib_recv.at[1], sibling)

    with scope("panels_1"):
        panels.landed(1, -1)
        panels.passed(0)
    with scope("first_factor_y"):
        fa_own.wait()
        for distance in (1, 3, 2):
            remote(
                ft.at[:, y, x],
                ft.at[:, (y + 4 - distance) % 4, x],
                fa_send.at[distance - 1],
                fa_recv.at[distance - 1],
                sibling,
            ).wait_recv()
    f_gather.start()
    with scope("coupling_z"):
        for which in (0, 1):

            @pl.when(z == 2 + which)
            def _():
                fz_own.wait()

            @pl.when(z != 2 + which)
            def _():
                remote(
                    fz_src, fz_dst(which), fz_send.at[0], fz_recv.at[which], sibling
                ).wait_recv()

    fxy.start()
    with scope("second_coupling_z"):

        @pl.when(z == 1)
        def _():
            gz_own.wait()

        @pl.when(z != 1)
        def _():
            remote(gz_src, gz_dst, gz_send.at[0], gz_recv.at[0], sibling).wait_recv()

    gxy.start()
    with scope("panels_2"):
        panels.landed(2, -2)
        panels.passed(1, -1)
    with scope("pass_coupling_y"):
        fxy.forward()
        gxy.forward()
    with scope("panels_3"):
        panels.landed(3, -3)
        panels.passed(2, -2)
    with scope("finish_coupling_y"):
        fxy.finish()
    fxx.start()
    with scope("pass_first_factor"):
        f_gather.forward()
    with scope("panels_4"):
        panels.landed(4)
        panels.passed(3, -3)
    with scope("finish_second_coupling_y"):
        gxy.finish()
    gxx.start()
    with scope("pass_coupling_x"):
        fxx.forward()
    with scope("second_factor_x"):

        @pl.when(g_source(z))
        def _():
            for source_x in range(4):
                stays = jnp.logical_and(source_x == x, k == x % 2)
                block = gt.at[z // 2 - 1, k, y, source_x]

                @pl.when(stays)
                def _():
                    pltpu.make_async_copy(factor2.at[k], block, local.at[7]).wait()

                @pl.when(jnp.logical_not(stays))
                def _():
                    remote(
                        block, block, ga_send.at[0], ga_recv.at[source_x, x % 2], sibling
                    ).wait_recv()

    seconds.landed(0, over=False)
    with scope("pass_panels_4"):
        panels.passed(4)
    xa_own.start()

    @pl.when(y == 0)
    def _():
        for distance in (2, 1, 3):
            xa_copy(distance).start()

    @pl.when(y != 0)
    def _():
        for distance in (2, 1, 3):
            xa_copy(distance).start()

    with scope("finish_first_factor"):
        f_gather.finish()

    has_panel_rows = jnp.logical_and(y == 0, r < 8)
    with scope("turn_first_factor"):
        for panel in (0, 1):
            for part in range(4):
                high, rest = split(ft[panel, part].reshape(128, 384).T)
                at = (4 * panel + part) * 128
                wh[:, at : at + 128] = high
                wl[:, at : at + 128] = rest

        @pl.when(has_panel_rows)
        def _():
            row = lax.broadcasted_iota(jnp.int32, (128, 1024), 0)
            column = lax.broadcasted_iota(jnp.int32, (128, 1024), 1)
            unit = jnp.where(column == row + r * 128, -1.0, 0.0)
            wh[pl.ds(0, 128), :] = unit.astype(BF16)
            wl[pl.ds(0, 128), :] = jnp.zeros((128, 1024), BF16)

    with scope("finish_coupling_x"):
        fxx.finish()
    fx_to_sibling.start()
    with scope("pass_second_coupling_x"):
        gxx.forward()
    with scope("seconds_1"):
        seconds.landed(1, -1, over=False)
    with scope("arrived_panels_1"):
        panels.arrived(0, 1, -1)
    with scope("coupling_core"):
        load1.wait()
        fx_from_sibling.wait_recv()

    with scope("left_operator"):
        value1 = split(product((wh[:, 512:], wl[:, 512:]), split(i1[1])))
        vh[:, 512:], vl[:, 512:] = value1
        value0 = wh[:, :512].astype(F32) + wl[:, :512].astype(F32)
        for number in range(4):
            at = 512 + 128 * number
            value0 = value0 - product(
                (vh[:, at : at + 128], vl[:, at : at + 128]),
                split(fx[number % 2, number // 2].reshape(512, 128)),
                NT,
            )
        vh[:, :512], vl[:, :512] = split(product(split(value0), split(i1[0])))

    load2 = pltpu.make_async_copy(inverse2, i1, local.at[6])
    load2.start()
    with scope("finish_second_coupling_x"):
        gxx.finish()
    gx_to_sibling.start()
    with scope("arrived_panels_2"):
        panels.arrived(2, -2, 3, -3, 4)
    with scope("seconds_2"):
        seconds.landed(2, -2, over=False)
    seconds.go_over(0, 1, -1, 2, -2)

    def wait_slab(distance):
        remote(
            xt.at[y],
            xt.at[(y + 4 - distance) % 4],
            xa_send.at[distance - 1],
            xa_recv.at[distance - 1],
            sibling,
        ).wait_recv()

    def left(block):
        rows = split(xp[block].reshape(1024, 256))
        return xt[block] - product((vh[...], vl[...]), rows)

    with scope("wait_slab_0"):
        for distance in (1, 2, 3):

            @pl.when(y == distance)
            def _():
                wait_slab(distance)

        @pl.when(y == 0)
        def _():
            xa_own.wait()

    with scope("wait_panels_core"):
        @pl.when(in_panels(z))
        def _():
            own_panel().wait()

        for number in range(4):
            for source in range(4):
                panels.wait_core(number, source)

    @pl.when(has_panel_rows)
    def _():
        xt[0, pl.ds(0, 128)] = jnp.zeros((128, 256), F32)

    with scope("left_update_0"):
        pb[x] = left(0)

    p_gather = Gather4(
        x,
        along_x,
        lambda index: pb.at[index],
        lambda part, index: pb.at[index, pl.ds(192 * part, 192)],
        p_send,
        p_recv,
    )
    p_gather.start()
    with scope("seconds_3"):
        seconds.landed(3, -3)
    with scope("wait_right_operator"):
        load2.wait()
        gx_from_sibling.wait_recv()
    with scope("right_operator"):
        for panel in (0, 1):
            i2h[panel], i2l[panel] = split(i1[panel])
        total = None
        for part in (0, 1):
            at = 256 * part
            term = product(
                (i2h[1, :, at : at + 256], i2l[1, :, at : at + 256]),
                split(gx[part].reshape(512, 256)),
                NT,
            )
            total = term if total is None else total + term
        kh[...], kl[...] = split(product(split(total), (i2h[0], i2l[0])))

    with scope("seconds_4"):
        seconds.landed(4)
    with scope("pass_seconds_0"):
        seconds.passed(0, 1, -1)
    with scope("pass_columns"):
        p_gather.forward()
    with scope("wait_slab_rest"):
        for distance in (1, 2, 3):

            @pl.when(y != distance)
            def _():
                wait_slab(distance)

        @pl.when(y != 0)
        def _():
            xa_own.wait()

        @pl.when(has_panel_rows)
        def _():
            for block in range(1, 4):
                xt[block, pl.ds(0, 128)] = jnp.zeros((128, 256), F32)

    with scope("pass_seconds"):
        seconds.passed(2, -2)
    with scope("left_update_rest"):

        @pl.loop(1, 4)
        def _(block):
            db[block] = left(block)

    with scope("pass_seconds"):
        seconds.passed(3, -3, 4)
    with scope("arrived_seconds"):
        seconds.arrived(*EVENTS)
    with scope("finish_columns"):
        p_gather.finish()

    with scope("solve_columns"):
        for half in (0, 1):
            rows = pl.ds(256 * half, 256)
            first = None
            second = None
            for part in range(2):
                at = 256 * part
                left0 = split(pb[part])
                left1 = split(pb[2 + part])
                term0 = product(left0, (i2h[0, rows, at : at + 256], i2l[0, rows, at : at + 256]), NT)
                term1 = product(
                    left1, (i2h[1, rows, at : at + 256], i2l[1, rows, at : at + 256]), NT
                ) - product(left0, (kh[rows, at : at + 256], kl[rows, at : at + 256]), NT)
                first = term0 if first is None else first + term0
                second = term1 if second is None else second + term1
            for number, value in ((half, first), (2 + half, second)):
                at = 256 * number
                zh[:, at : at + 256], zl[:, at : at + 256] = split(value)

                @pl.when(x == number)
                def _():
                    db[0] = value

    out_rows = out.at[pl.ds(pl.multiple_of(r * 96, 32), 96), :]

    def own_rows_of(block):
        return db.at[block, pl.ds(pl.multiple_of(96 * x, 32), 96)]

    def turn_x(block, distance):
        to = (x + distance) % 4
        return remote(
            db.at[block, pl.ds(pl.multiple_of(96 * to, 32), 96)],
            eb.at[x, block],
            e_send.at[block, distance - 1],
            e_recv.at[block, distance - 1],
            along_x(to),
        )

    def turn_z(block, distance, remote_do, local_do):
        from_x = (x + 4 - distance) % 4
        src = own_rows_of(block) if distance == 0 else eb.at[from_x, block]
        to = 4 * block + from_x

        @pl.when(to == r)
        def _():
            local_do(pltpu.make_async_copy(src, out_rows, local.at[8]))

        @pl.when(to != r)
        def _():
            remote_do(
                remote(src, out_rows, o_send.at[block, distance], o_recv.at[r], (to, c))
            )

    def start(copy):
        copy.start()

    with scope("seconds_core"):
        for number in range(4):
            for block in range(3):
                seconds.wait_core(number, 2 * block + 2)
    with scope("right_update"):
        for turn in (2, 1, 3, 0):
            block = (z // 2 + turn) % 4

            @pl.when(block != 0)
            def _():
                factor = split(gt[block - 1].reshape(1024, 256))
                db[block] = db[block] - product((zh[...], zl[...]), factor)

            for distance in (2, 1, 3):
                turn_x(block, distance).start()
            turn_z(block, 0, start, start)
    with scope("pass_out"):
        for turn in (2, 1, 3, 0):
            block = (z // 2 + turn) % 4
            for distance in (1, 3, 2):
                here = eb.at[(x + 4 - distance) % 4, block]
                remote(
                    here,
                    here,
                    e_send.at[block, distance - 1],
                    e_recv.at[block, distance - 1],
                    sibling,
                ).wait_recv()
                turn_z(block, distance, start, start)

    with scope("wait_out"):
        for source in range(16):
            rows = out.at[pl.ds(96 * source, 96), :]

            @pl.when(source != r)
            def _():
                remote(rows, rows, o_send.at[0, 0], o_recv.at[source], sibling).wait_recv()

    with scope("drain"):
        for block in range(4):
            for distance in range(4):
                turn_z(block, distance, lambda copy: copy.wait_send(), lambda copy: copy.wait())
            for distance in (1, 2, 3):
                turn_x(block, distance).wait_send()
        panels.sent()
        seconds.sent()

        @pl.when(f_source)
        def _():
            for distance in range(1, 8):
                fz_copy(distance).wait_send()

        @pl.when(z == 1)
        def _():
            for distance in range(1, 8):
                gz_copy(distance).wait_send()

        for distance in (1, 2, 3):
            fa_copy(distance).wait_send()
            xa_copy(distance).wait_send()
        for panel in (0, 1):

            @pl.when(jnp.logical_and(z >= 2, jnp.logical_not(ga_stays(panel))))
            def _():
                ga_copy(panel).wait_send()

        for gather in (fxx, fxy, gxx, gxy, f_gather, p_gather):
            gather.drain()
        fx_to_sibling.wait_send()
        gx_to_sibling.wait_send()


def on_device(*arrays):
    dma = pltpu.SemaphoreType.DMA
    any_space = pl.BlockSpec(memory_space=pl.ANY)
    scratch = [
        pltpu.VMEM((2, 512, 512), F32),
        pltpu.VMEM((2, 512, 512), BF16),
        pltpu.VMEM((2, 512, 512), BF16),
        pltpu.VMEM((512, 512), BF16),
        pltpu.VMEM((512, 512), BF16),
        pltpu.VMEM((4, 384, 256), F32),
        pltpu.VMEM((4, 8, 128, 256), F32),
        pltpu.VMEM((2, 2, 4, 4, 32, 128), F32),
        pltpu.VMEM((2, 4, 4, 32, 256), F32),
        pltpu.VMEM((2, 4, 4, 32, 384), F32),
        pltpu.VMEM((384, 1024), BF16),
        pltpu.VMEM((384, 1024), BF16),
        pltpu.VMEM((384, 1024), BF16),
        pltpu.VMEM((384, 1024), BF16),
        pltpu.VMEM((3, 2, 4, 4, 32, 256), F32),
        pltpu.VMEM((4, 384, 256), F32),
        pltpu.VMEM((384, 1024), BF16),
        pltpu.VMEM((384, 1024), BF16),
        pltpu.VMEM((4, 384, 256), F32),
        pltpu.VMEM((4, 4, 96, 256), F32),
        dma((9,)),
        dma((4,)),
        dma((4,)),
        dma((4,)),
        dma((4,)),
        dma((4, 4)),
        dma((4, 4)),
        dma((4, 4)),
        dma((4, 4)),
        dma((7,)),
        dma((2,)),
        dma((7,)),
        dma((1,)),
        dma((4,)),
        dma((4,)),
        dma((4,)),
        dma((4,)),
        dma((4,)),
        dma((4,)),
        dma((4,)),
        dma((4,)),
        dma((2,)),
        dma((2,)),
        dma((3,)),
        dma((3,)),
        dma((4,)),
        dma((4,)),
        dma((3,)),
        dma((3,)),
        dma((2,)),
        dma((4, 2)),
        dma((8,)),
        dma((8,)),
        dma((8,)),
        dma((8,)),
        dma((3, 4)),
        dma((3, 4)),
        dma((4, 3)),
        dma((4, 3)),
        dma((4,)),
        dma((4,)),
        dma((4, 3)),
        dma((4, 3)),
        dma((4, 4)),
        dma((16,)),
    ]
    return pl.pallas_call(
        kernel,
        out_shape=jax.ShapeDtypeStruct((1536, 256), F32),
        in_specs=[any_space] * 5,
        out_specs=any_space,
        scratch_shapes=scratch,
        compiler_params=pltpu.CompilerParams(
            has_side_effects=True, collective_id=0, vmem_limit_bytes=56 * 1024 * 1024
        ),
        name="two_sided_panels",
    )(*arrays)


def solution(mesh):
    return jax.shard_map(
        on_device,
        mesh=mesh,
        in_specs=(P("rows", "cols"), P(), P(None, "cols", "rows"), P(), P(None, "cols", "rows")),
        out_specs=P("cols", "rows"),
        check_vma=False,
    )
```

```python
import jax
import jax.numpy as jnp
from jax import lax
from jax.experimental import pallas as pl
from jax.experimental.pallas import tpu as pltpu
from jax.sharding import PartitionSpec as P

MESH = pl.DeviceIdType.MESH
F32 = jnp.float32
BF16 = jnp.bfloat16
NN = (((1,), (0,)), ((), ()))
NT = (((1,), (1,)), ((), ()))


def split(value):
    high = value.astype(BF16)
    return high, (value - high.astype(F32)).astype(BF16)


def product(a, b, dims=NN):
    def dot(u, v):
        return lax.dot_general(u, v, dims, preferred_element_type=F32)

    return dot(a[0], b[0]) + (dot(a[0], b[1]) + dot(a[1], b[0]))


def remote(src, dst, send_sem, recv_sem, device):
    return pltpu.make_async_remote_copy(
        src_ref=src,
        dst_ref=dst,
        send_sem=send_sem,
        recv_sem=recv_sem,
        device_id=device,
        device_id_type=MESH,
    )


class Gather4:
    def __init__(self, index, device, slot, half, send, recv, src=None):
        self.up, self.down, self.far = (index + 1) % 4, (index + 3) % 4, (index + 2) % 4
        self.slot = slot
        to_up, to_down = device(self.up), device(self.down)
        own = slot(index)
        self.first = [
            remote(own if src is None else src, own, send.at[0], recv.at[0], to_up),
            remote(own if src is None else src, own, send.at[1], recv.at[1], to_down),
        ]
        self.second = [
            remote(half(0, self.down), half(0, self.down), send.at[2], recv.at[2], to_up),
            remote(half(1, self.up), half(1, self.up), send.at[3], recv.at[3], to_down),
        ]
        self.landing = [
            remote(own, slot(self.down), send.at[0], recv.at[0], to_up),
            remote(own, slot(self.up), send.at[1], recv.at[1], to_down),
            remote(half(0, self.far), half(0, self.far), send.at[2], recv.at[2], to_up),
            remote(half(1, self.far), half(1, self.far), send.at[3], recv.at[3], to_down),
        ]

    def start(self):
        for copy in self.first:
            copy.start()

    def forward(self, then=None):
        for way in (0, 1):
            self.landing[way].wait_recv()
            self.second[way].start()
            if then is not None:
                then(way, (self.down, self.up)[way])

    def finish(self, then=None):
        self.landing[2].wait_recv()
        self.landing[3].wait_recv()
        if then is not None:
            then(2, self.far)

    def drain(self):
        for copy in self.first + self.second:
            copy.wait_send()


class Spread8:
    def __init__(self, z, device, is_source, block, up, down):
        self.z, self.is_source, self.block, self.up, self.down = z, is_source, block, up, down
        self.above, self.below = device((z + 1) % 8), device((z + 7) % 8)

    def source(self, event):
        return (self.z + 16 - event) % 8

    def copy(self, way, source, src=None):
        block = self.block(source)
        send, recv = self.up if way > 0 else self.down
        to = self.above if way > 0 else self.below
        return remote(
            block if src is None else src, block, send.at[source], recv.at[source], to
        )

    def landed(self, event, then=None, src=None):
        source = self.source(event)

        @pl.when(self.is_source(source))
        def _():
            if event != 0:
                self.copy(1 if event > 0 else -1, source).wait_recv()
            if 0 <= event < 4:
                self.copy(1, source, src).start()
            if -3 < event <= 0:
                self.copy(-1, source, src).start()
            if then is not None:
                then(source)

    def sent(self, event, then=None):
        source = self.source(event)

        @pl.when(self.is_source(source))
        def _():
            if 0 <= event < 4:
                self.copy(1, source).wait_send()
            if -3 < event <= 0:
                self.copy(-1, source).wait_send()
            if then is not None:
                then(source)


EVENTS = (0, 1, -1, 2, -2, 3, -3, 4)


class Flow:
    def __init__(self, z, y, k, is_source, key, block, half, devices, sems):
        self.z, self.y, self.k, self.is_source, self.key = z, y, k, is_source, key
        self.block, self.half = block, half
        self.along_y, self.sibling = devices[1], devices[2]
        self.up, self.down, self.over, self.core = sems
        self.spread = Spread8(
            z,
            devices[0],
            is_source,
            lambda source: block(y, source, k),
            self.up,
            self.down,
        )

    def indices(self):
        return self.y, (self.y + 3) % 4, (self.y + 1) % 4, (self.y + 2) % 4

    def gather(self, source, src=None):
        key = self.key(source)
        return Gather4(
            self.y,
            self.along_y,
            lambda index: self.block(index, source, self.k),
            lambda part, index: self.half(part, index, source),
            self.over[0].at[key],
            self.over[1].at[key],
            src,
        )

    def to_core(self, number, source, core, src=None):
        block = self.block(self.indices()[number], source, core)
        send, recv = self.core
        key = self.key(source)
        return remote(
            block if src is None else src,
            block,
            send.at[number, key],
            recv.at[number, key],
            self.sibling,
        )

    def landed(self, *events, src=None, over=True):
        def then(source):
            if over:
                self.gather(source, src).start()
            self.to_core(0, source, self.k, src).start()

        for event in events:
            self.spread.landed(event, then, src)

    def go_over(self, *events):
        for event in events:
            source = self.spread.source(event)

            @pl.when(self.is_source(source))
            def _():
                self.gather(source).start()

    def passed(self, *events):
        for event in events:
            source = self.spread.source(event)

            @pl.when(self.is_source(source))
            def _():
                self.gather(source).forward(
                    then=lambda number, index: self.to_core(1 + number, source, self.k).start()
                )

    def arrived(self, *events):
        for event in events:
            source = self.spread.source(event)

            @pl.when(self.is_source(source))
            def _():
                self.gather(source).finish(
                    then=lambda number, index: self.to_core(1 + number, source, self.k).start()
                )

    def wait_core(self, number, source):
        self.to_core(number, source, 1 - self.k).wait_recv()

    def sent(self):
        def then(source):
            self.gather(source).drain()
            for number in range(4):
                self.to_core(number, source, self.k).wait_send()

        for event in EVENTS:
            self.spread.sent(event, then)


def kernel(
    slab,
    inverse1,
    factor1,
    inverse2,
    factor2,
    out,
    i1,
    i2h,
    i2l,
    kh,
    kl,
    xt,
    xp,
    fx,
    gx,
    ft,
    wh,
    wl,
    vh,
    vl,
    gt,
    pb,
    zh,
    zl,
    db,
    eb,
    local,
    up_send,
    up_recv,
    down_send,
    down_recv,
    py_send,
    py_recv,
    xs_send,
    xs_recv,
    fz_send,
    fz_recv,
    gz_send,
    gz_recv,
    fxx_send,
    fxx_recv,
    fxy_send,
    fxy_recv,
    gxx_send,
    gxx_recv,
    gxy_send,
    gxy_recv,
    sib_send,
    sib_recv,
    fa_send,
    fa_recv,
    ft_send,
    ft_recv,
    xa_send,
    xa_recv,
    ga_send,
    ga_recv,
    gu_send,
    gu_recv,
    gd_send,
    gd_recv,
    gy_send,
    gy_recv,
    gs_send,
    gs_recv,
    p_send,
    p_recv,
    e_send,
    e_recv,
    o_send,
    o_recv,
):
    r = lax.axis_index("rows")
    c = lax.axis_index("cols")
    z, k = r // 2, r % 2
    y, x = c // 4, c % 4
    sibling = (2 * z + 1 - k, c)
    scope = jax.named_scope

    def along_y(index):
        return (r, 4 * index + x)

    def along_x(index):
        return (r, 4 * y + index)

    def along_z(index):
        return (2 * index + k, c)

    panel_rows = slab.at[pl.ds(0, 128), :]

    def in_panels(source):
        return source < 4

    panels = Flow(
        z,
        y,
        k,
        in_panels,
        lambda source: source,
        lambda index, source, core: xp.at[index, 2 * source + core],
        lambda part, index, source: xp.at[index, 2 * source + k, pl.ds(64 * part, 64)],
        (along_z, along_y, sibling),
        ((up_send, up_recv), (down_send, down_recv), (py_send, py_recv), (xs_send, xs_recv)),
    )

    def own_panel():
        return pltpu.make_async_copy(panel_rows, xp.at[y, 2 * z + k], local.at[0])

    with scope("barrier"):
        barrier = pltpu.get_barrier_semaphore()
        for distance in range(1, 4):
            over_x = (x + distance) % 4
            for device in (
                along_y((y + distance) % 4),
                along_x(over_x),
                (2 * z + 1 - k, 4 * y + over_x),
            ):
                pl.semaphore_signal(barrier, inc=1, device_id=device, device_id_type=MESH)
        for distance in range(1, 16):
            pl.semaphore_signal(
                barrier, inc=1, device_id=((r + distance) % 16, c), device_id_type=MESH
            )
        pl.semaphore_wait(barrier, 24)

    panels.landed(0, src=panel_rows)

    @pl.when(in_panels(z))
    def _():
        own_panel().start()

    fz_src = factor1.at[0, :, pl.ds(0, 128)]
    gz_src = factor2.at[0]

    def fz_dst(which):
        return fx.at[k, which, y, x]

    gz_dst = gx.at[k, y, x]
    fz_own = pltpu.make_async_copy(fz_src, fz_dst(z % 2), local.at[1])
    gz_own = pltpu.make_async_copy(gz_src, gz_dst, local.at[2])
    f_source = jnp.logical_or(z == 2, z == 3)

    def fz_copy(distance):
        return remote(
            fz_src,
            fz_dst(z % 2),
            fz_send.at[distance - 1],
            fz_recv.at[z % 2],
            along_z((z + distance) % 8),
        )

    def gz_copy(distance):
        return remote(
            gz_src, gz_dst, gz_send.at[distance - 1], gz_recv.at[0], along_z((z + distance) % 8)
        )

    @pl.when(f_source)
    def _():
        fz_own.start()
        for distance in range(1, 8):
            fz_copy(distance).start()

    def fa_copy(distance):
        to = (y + distance) % 4
        columns = pl.ds(pl.multiple_of(to * 384, 128), 384)
        return remote(
            factor1.at[:, :, columns],
            ft.at[:, y, x],
            fa_send.at[distance - 1],
            fa_recv.at[distance - 1],
            along_y(to),
        )

    fa_own = pltpu.make_async_copy(
        factor1.at[:, :, pl.ds(pl.multiple_of(y * 384, 128), 384)], ft.at[:, y, x], local.at[3]
    )
    fa_own.start()
    for distance in (2, 1, 3):
        fa_copy(distance).start()

    load1 = pltpu.make_async_copy(inverse1, i1, local.at[5])
    load1.start()

    @pl.when(z == 1)
    def _():
        gz_own.start()
        for distance in range(1, 8):
            gz_copy(distance).start()

    g_plane = r % 4
    g_block = r // 4

    def ga_copy(panel):
        return remote(
            factor2.at[panel],
            gt.at[g_block - 1, panel, y, x],
            ga_send.at[panel],
            ga_recv.at[x, k],
            (2 * z + panel, 4 * y + g_plane),
        )

    def ga_own(panel):
        return pltpu.make_async_copy(
            factor2.at[panel], gt.at[g_block - 1, panel, y, x], local.at[7]
        )

    def ga_stays(panel):
        return jnp.logical_and(g_plane == x, k == panel)

    for panel in (0, 1):

        @pl.when(jnp.logical_and(z >= 2, ga_stays(panel)))
        def _():
            ga_own(panel).start()

        @pl.when(jnp.logical_and(z >= 2, jnp.logical_not(ga_stays(panel))))
        def _():
            ga_copy(panel).start()

    def g_source(source):
        return jnp.logical_and(source >= 2, source % 2 == x // 2)

    seconds = Flow(
        z,
        y,
        k,
        g_source,
        lambda source: source // 2 - 1,
        lambda index, source, core: gt.at[source // 2 - 1, core, index],
        lambda part, index, source: gt.at[source // 2 - 1, k, index, pl.ds(2 * part, 2)],
        (along_z, along_y, sibling),
        ((gu_send, gu_recv), (gd_send, gd_recv), (gy_send, gy_recv), (gs_send, gs_recv)),
    )

    def xa_copy(distance):
        to = (y + distance) % 4
        return remote(
            slab.at[pl.ds(pl.multiple_of(to * 384, 128), 384), :],
            xt.at[y],
            xa_send.at[distance - 1],
            xa_recv.at[distance - 1],
            along_y(to),
        )

    xa_own = pltpu.make_async_copy(
        slab.at[pl.ds(pl.multiple_of(y * 384, 128), 384), :], xt.at[y], local.at[4]
    )

    fxy = Gather4(
        y,
        along_y,
        lambda index: fx.at[k, :, index, x],
        lambda part, index: fx.at[k, part, index, x],
        fxy_send,
        fxy_recv,
    )
    fxx = Gather4(
        x,
        along_x,
        lambda index: fx.at[k, :, :, index],
        lambda part, index: fx.at[k, part, :, index],
        fxx_send,
        fxx_recv,
    )
    gxy = Gather4(
        y,
        along_y,
        lambda index: gx.at[k, index, x],
        lambda part, index: gx.at[k, index, x, pl.ds(16 * part, 16)],
        gxy_send,
        gxy_recv,
    )
    gxx = Gather4(
        x,
        along_x,
        lambda index: gx.at[k, :, index],
        lambda part, index: gx.at[k, pl.ds(2 * part, 2), index],
        gxx_send,
        gxx_recv,
    )
    f_gather = Gather4(
        x,
        along_x,
        lambda index: ft.at[:, :, index],
        lambda part, index: ft.at[part, :, index],
        ft_send,
        ft_recv,
    )
    fx_to_sibling = remote(fx.at[k], fx.at[k], sib_send.at[0], sib_recv.at[0], sibling)
    gx_to_sibling = remote(gx.at[k], gx.at[k], sib_send.at[1], sib_recv.at[1], sibling)
    fx_from_sibling = remote(fx.at[1 - k], fx.at[1 - k], sib_send.at[0], sib_recv.at[0], sibling)
    gx_from_sibling = remote(gx.at[1 - k], gx.at[1 - k], sib_send.at[1], sib_recv.at[1], sibling)

    with scope("panels_1"):
        panels.landed(1, -1)
        panels.passed(0)
    with scope("first_factor_y"):
        fa_own.wait()
        for distance in (1, 3, 2):
            remote(
                ft.at[:, y, x],
                ft.at[:, (y + 4 - distance) % 4, x],
                fa_send.at[distance - 1],
                fa_recv.at[distance - 1],
                sibling,
            ).wait_recv()
    f_gather.start()
    with scope("coupling_z"):
        for which in (0, 1):

            @pl.when(z == 2 + which)
            def _():
                fz_own.wait()

            @pl.when(z != 2 + which)
            def _():
                remote(
                    fz_src, fz_dst(which), fz_send.at[0], fz_recv.at[which], sibling
                ).wait_recv()

    fxy.start()
    with scope("second_coupling_z"):

        @pl.when(z == 1)
        def _():
            gz_own.wait()

        @pl.when(z != 1)
        def _():
            remote(gz_src, gz_dst, gz_send.at[0], gz_recv.at[0], sibling).wait_recv()

    gxy.start()
    with scope("panels_2"):
        panels.landed(2, -2)
        panels.passed(1, -1)
    with scope("pass_coupling_y"):
        fxy.forward()
        gxy.forward()
    with scope("panels_3"):
        panels.landed(3, -3)
        panels.passed(2, -2)
    with scope("finish_coupling_y"):
        fxy.finish()
    fxx.start()
    with scope("pass_first_factor"):
        f_gather.forward()
    with scope("panels_4"):
        panels.landed(4)
        panels.passed(3, -3)
    with scope("finish_second_coupling_y"):
        gxy.finish()
    gxx.start()
    with scope("pass_coupling_x"):
        fxx.forward()
    with scope("second_factor_x"):

        @pl.when(g_source(z))
        def _():
            for source_x in range(4):
                stays = jnp.logical_and(source_x == x, k == x % 2)
                block = gt.at[z // 2 - 1, k, y, source_x]

                @pl.when(stays)
                def _():
                    pltpu.make_async_copy(factor2.at[k], block, local.at[7]).wait()

                @pl.when(jnp.logical_not(stays))
                def _():
                    remote(
                        block, block, ga_send.at[0], ga_recv.at[source_x, x % 2], sibling
                    ).wait_recv()

    seconds.landed(0, over=False)
    with scope("pass_panels_4"):
        panels.passed(4)
    xa_own.start()

    @pl.when(y == 0)
    def _():
        for distance in (2, 1, 3):
            xa_copy(distance).start()

    @pl.when(y != 0)
    def _():
        for distance in (2, 1, 3):
            xa_copy(distance).start()

    with scope("finish_first_factor"):
        f_gather.finish()

    has_panel_rows = jnp.logical_and(y == 0, r < 8)
    with scope("turn_first_factor"):
        for panel in (0, 1):
            for part in range(4):
                high, rest = split(ft[panel, part].reshape(128, 384).T)
                at = (4 * panel + part) * 128
                wh[:, at : at + 128] = high
                wl[:, at : at + 128] = rest

        @pl.when(has_panel_rows)
        def _():
            row = lax.broadcasted_iota(jnp.int32, (128, 1024), 0)
            column = lax.broadcasted_iota(jnp.int32, (128, 1024), 1)
            unit = jnp.where(column == row + r * 128, -1.0, 0.0)
            wh[pl.ds(0, 128), :] = unit.astype(BF16)
            wl[pl.ds(0, 128), :] = jnp.zeros((128, 1024), BF16)

    with scope("finish_coupling_x"):
        fxx.finish()
    fx_to_sibling.start()
    with scope("pass_second_coupling_x"):
        gxx.forward()
    with scope("seconds_1"):
        seconds.landed(1, -1, over=False)
    with scope("arrived_panels_1"):
        panels.arrived(0, 1, -1)
    with scope("coupling_core"):
        load1.wait()
        fx_from_sibling.wait_recv()

    with scope("left_operator"):
        value1 = split(product((wh[:, 512:], wl[:, 512:]), split(i1[1])))
        vh[:, 512:], vl[:, 512:] = value1
        value0 = wh[:, :512].astype(F32) + wl[:, :512].astype(F32)
        for number in range(4):
            at = 512 + 128 * number
            value0 = value0 - product(
                (vh[:, at : at + 128], vl[:, at : at + 128]),
                split(fx[number % 2, number // 2].reshape(512, 128)),
                NT,
            )
        vh[:, :512], vl[:, :512] = split(product(split(value0), split(i1[0])))

    load2 = pltpu.make_async_copy(inverse2, i1, local.at[6])
    load2.start()
    with scope("finish_second_coupling_x"):
        gxx.finish()
    gx_to_sibling.start()
    with scope("arrived_panels_2"):
        panels.arrived(2, -2, 3, -3, 4)
    with scope("seconds_2"):
        seconds.landed(2, -2, over=False)
    seconds.go_over(0, 1, -1, 2, -2)

    def wait_slab(distance):
        remote(
            xt.at[y],
            xt.at[(y + 4 - distance) % 4],
            xa_send.at[distance - 1],
            xa_recv.at[distance - 1],
            sibling,
        ).wait_recv()

    def left(block):
        rows = split(xp[block].reshape(1024, 256))
        return xt[block] - product((vh[...], vl[...]), rows)

    with scope("wait_slab_0"):
        for distance in (1, 2, 3):

            @pl.when(y == distance)
            def _():
                wait_slab(distance)

        @pl.when(y == 0)
        def _():
            xa_own.wait()

    with scope("wait_panels_core"):
        @pl.when(in_panels(z))
        def _():
            own_panel().wait()

        for number in range(4):
            for source in range(4):
                panels.wait_core(number, source)

    @pl.when(has_panel_rows)
    def _():
        xt[0, pl.ds(0, 128)] = jnp.zeros((128, 256), F32)

    with scope("left_update_0"):
        pb[x] = left(0)

    p_gather = Gather4(
        x,
        along_x,
        lambda index: pb.at[index],
        lambda part, index: pb.at[index, pl.ds(192 * part, 192)],
        p_send,
        p_recv,
    )
    p_gather.start()
    with scope("seconds_3"):
        seconds.landed(3, -3)
    with scope("wait_right_operator"):
        load2.wait()
        gx_from_sibling.wait_recv()
    with scope("right_operator"):
        for panel in (0, 1):
            i2h[panel], i2l[panel] = split(i1[panel])
        total = None
        for part in (0, 1):
            at = 256 * part
            term = product(
                (i2h[1, :, at : at + 256], i2l[1, :, at : at + 256]),
                split(gx[part].reshape(512, 256)),
                NT,
            )
            total = term if total is None else total + term
        kh[...], kl[...] = split(product(split(total), (i2h[0], i2l[0])))

    with scope("seconds_4"):
        seconds.landed(4)
    with scope("pass_seconds_0"):
        seconds.passed(0, 1, -1)
    with scope("pass_columns"):
        p_gather.forward()
    with scope("wait_slab_rest"):
        for distance in (1, 2, 3):

            @pl.when(y != distance)
            def _():
                wait_slab(distance)

        @pl.when(y != 0)
        def _():
            xa_own.wait()

        @pl.when(has_panel_rows)
        def _():
            for block in range(1, 4):
                xt[block, pl.ds(0, 128)] = jnp.zeros((128, 256), F32)

    with scope("pass_seconds"):
        seconds.passed(2, -2)
    with scope("left_update_rest"):

        @pl.loop(1, 4)
        def _(block):
            db[block] = left(block)

    with scope("pass_seconds"):
        seconds.passed(3, -3, 4)
    with scope("finish_columns"):
        p_gather.finish()

    with scope("solve_columns"):
        for half in (0, 1):
            rows = pl.ds(256 * half, 256)
            first = None
            second = None
            for part in range(2):
                at = 256 * part
                left0 = split(pb[part])
                left1 = split(pb[2 + part])
                term0 = product(left0, (i2h[0, rows, at : at + 256], i2l[0, rows, at : at + 256]), NT)
                term1 = product(
                    left1, (i2h[1, rows, at : at + 256], i2l[1, rows, at : at + 256]), NT
                ) - product(left0, (kh[rows, at : at + 256], kl[rows, at : at + 256]), NT)
                first = term0 if first is None else first + term0
                second = term1 if second is None else second + term1
            for number, value in ((half, first), (2 + half, second)):
                at = 256 * number
                zh[:, at : at + 256], zl[:, at : at + 256] = split(value)

                @pl.when(x == number)
                def _():
                    db[0] = value

    out_rows = out.at[pl.ds(pl.multiple_of(r * 96, 32), 96), :]

    def own_rows_of(block):
        return db.at[block, pl.ds(pl.multiple_of(96 * x, 32), 96)]

    def turn_x(block, distance):
        to = (x + distance) % 4
        return remote(
            db.at[block, pl.ds(pl.multiple_of(96 * to, 32), 96)],
            eb.at[x, block],
            e_send.at[block, distance - 1],
            e_recv.at[block, distance - 1],
            along_x(to),
        )

    def turn_z(block, distance, remote_do, local_do):
        from_x = (x + 4 - distance) % 4
        src = own_rows_of(block) if distance == 0 else eb.at[from_x, block]
        to = 4 * block + from_x

        @pl.when(to == r)
        def _():
            local_do(pltpu.make_async_copy(src, out_rows, local.at[8]))

        @pl.when(to != r)
        def _():
            remote_do(
                remote(src, out_rows, o_send.at[block, distance], o_recv.at[r], (to, c))
            )

    def start(copy):
        copy.start()

    with scope("arrived_seconds"):
        seconds.arrived(*EVENTS)
    with scope("seconds_core"):
        for number in range(4):
            for block in range(3):
                seconds.wait_core(number, 2 * block + 2)
    with scope("right_update"):
        for turn in (2, 1, 3, 0):
            block = (z // 2 + turn) % 4

            @pl.when(block != 0)
            def _():
                factor = split(gt[block - 1].reshape(1024, 256))
                db[block] = db[block] - product((zh[...], zl[...]), factor)

            for distance in (2, 1, 3):
                turn_x(block, distance).start()
            turn_z(block, 0, start, start)
    with scope("pass_out"):
        for turn in (2, 1, 3, 0):
            block = (z // 2 + turn) % 4
            for distance in (1, 3, 2):
                here = eb.at[(x + 4 - distance) % 4, block]
                remote(
                    here,
                    here,
                    e_send.at[block, distance - 1],
                    e_recv.at[block, distance - 1],
                    sibling,
                ).wait_recv()
                turn_z(block, distance, start, start)

    with scope("wait_out"):
        for source in range(16):
            rows = out.at[pl.ds(96 * source, 96), :]

            @pl.when(source != r)
            def _():
                remote(rows, rows, o_send.at[0, 0], o_recv.at[source], sibling).wait_recv()

    with scope("drain"):
        for block in range(4):
            for distance in range(4):
                turn_z(block, distance, lambda copy: copy.wait_send(), lambda copy: copy.wait())
            for distance in (1, 2, 3):
                turn_x(block, distance).wait_send()
        panels.sent()
        seconds.sent()

        @pl.when(f_source)
        def _():
            for distance in range(1, 8):
                fz_copy(distance).wait_send()

        @pl.when(z == 1)
        def _():
            for distance in range(1, 8):
                gz_copy(distance).wait_send()

        for distance in (1, 2, 3):
            fa_copy(distance).wait_send()
            xa_copy(distance).wait_send()
        for panel in (0, 1):

            @pl.when(jnp.logical_and(z >= 2, jnp.logical_not(ga_stays(panel))))
            def _():
                ga_copy(panel).wait_send()

        for gather in (fxx, fxy, gxx, gxy, f_gather, p_gather):
            gather.drain()
        fx_to_sibling.wait_send()
        gx_to_sibling.wait_send()


def on_device(*arrays):
    dma = pltpu.SemaphoreType.DMA
    any_space = pl.BlockSpec(memory_space=pl.ANY)
    scratch = [
        pltpu.VMEM((2, 512, 512), F32),
        pltpu.VMEM((2, 512, 512), BF16),
        pltpu.VMEM((2, 512, 512), BF16),
        pltpu.VMEM((512, 512), BF16),
        pltpu.VMEM((512, 512), BF16),
        pltpu.VMEM((4, 384, 256), F32),
        pltpu.VMEM((4, 8, 128, 256), F32),
        pltpu.VMEM((2, 2, 4, 4, 32, 128), F32),
        pltpu.VMEM((2, 4, 4, 32, 256), F32),
        pltpu.VMEM((2, 4, 4, 32, 384), F32),
        pltpu.VMEM((384, 1024), BF16),
        pltpu.VMEM((384, 1024), BF16),
        pltpu.VMEM((384, 1024), BF16),
        pltpu.VMEM((384, 1024), BF16),
        pltpu.VMEM((3, 2, 4, 4, 32, 256), F32),
        pltpu.VMEM((4, 384, 256), F32),
        pltpu.VMEM((384, 1024), BF16),
        pltpu.VMEM((384, 1024), BF16),
        pltpu.VMEM((4, 384, 256), F32),
        pltpu.VMEM((4, 4, 96, 256), F32),
        dma((9,)),
        dma((4,)),
        dma((4,)),
        dma((4,)),
        dma((4,)),
        dma((4, 4)),
        dma((4, 4)),
        dma((4, 4)),
        dma((4, 4)),
        dma((7,)),
        dma((2,)),
        dma((7,)),
        dma((1,)),
        dma((4,)),
        dma((4,)),
        dma((4,)),
        dma((4,)),
        dma((4,)),
        dma((4,)),
        dma((4,)),
        dma((4,)),
        dma((2,)),
        dma((2,)),
        dma((3,)),
        dma((3,)),
        dma((4,)),
        dma((4,)),
        dma((3,)),
        dma((3,)),
        dma((2,)),
        dma((4, 2)),
        dma((8,)),
        dma((8,)),
        dma((8,)),
        dma((8,)),
        dma((3, 4)),
        dma((3, 4)),
        dma((4, 3)),
        dma((4, 3)),
        dma((4,)),
        dma((4,)),
        dma((4, 3)),
        dma((4, 3)),
        dma((4, 4)),
        dma((16,)),
    ]
    return pl.pallas_call(
        kernel,
        out_shape=jax.ShapeDtypeStruct((1536, 256), F32),
        in_specs=[any_space] * 5,
        out_specs=any_space,
        scratch_shapes=scratch,
        compiler_params=pltpu.CompilerParams(
            has_side_effects=True, collective_id=0, vmem_limit_bytes=56 * 1024 * 1024
        ),
        name="two_sided_panels",
    )(*arrays)


def solution(mesh):
    return jax.shard_map(
        on_device,
        mesh=mesh,
        in_specs=(P("rows", "cols"), P(), P(None, "cols", "rows"), P(), P(None, "cols", "rows")),
        out_specs=P("cols", "rows"),
        check_vma=False,
    )
```
